32 devices in a mesh: segment: 2 (over core), clip: 4 (over z), tile: 4 (over y, x).
Axes of the slice: x: 2, y: 2, z: 4, core: 2. Of those that a mesh axis runs over, the one named last changes fastest.
Arguments:
- video: bfloat16 [4, 4, 3, 12, 4, 256], P('clip', 'tile'), may hold values from -6 to 6
- cotangent: bfloat16 [4, 4, 3, 12, 4, 256], P('clip', 'tile'), may hold values from -6 to 6
- weights: bfloat16 [2, 27, 256, 256], P('segment'), may hold values from -0.078125 to 0.078125
- neighbours: int32 [4, 4, 2], P('clip', 'tile'), may hold values from 0 to 4, as said below
- rows_used: int32 [4, 4], P('clip', 'tile'), may hold values from 3 to 12, as said below
- cols_used: int32 [4], P('clip'), may hold values from 2 to 4, as said below
Outputs:
- section_out: bfloat16 [2, 4, 4, 3, 12, 4, 256], P('segment', 'clip', 'tile')
- grads: float32 [2, 3, 589824], P('segment', None, ('clip', 'tile'))
The draws below stay inside these ranges and needn't reach their ends.
Inputs may be any that keep to these rules, and one draw needn't show every extreme that they name: `neighbours`: in each clip the strips of its frames lie on the 4 tiles in an order of their own: entry 0 names the tile of the strip above, entry 1 the tile of the strip below, 4 where there is none; exactly one strip of each clip has none above and one has none below, and the entries chain all 4 strips of a clip top to bottom. `rows_used`: in every clip some strip has 12 rows. `cols_used`: some clip has 4 columns.
All inputs are finite; a program needn't handle non-finite values.
Results may differ from the reference program's by a relative error of at most 0.0054.
Values may be sent and summed in bfloat16 or wider, within the bound.
A program may use at most 576 MiB of HBM per device.

```python
import jax
import jax.numpy as jnp
from jax import lax

CH = 256
FRAMES = 3
ROWS = 12
COLS = 4
TILES = 4
CLIPS = 4


def draw_neighbours(key, part):
    orders = jax.vmap(lambda single: jax.random.permutation(single, TILES))(jax.random.split(key, CLIPS)).astype(jnp.int32)
    clip_ids = jnp.arange(CLIPS, dtype=jnp.int32)[:, None]
    position = jnp.zeros((CLIPS, TILES), jnp.int32).at[clip_ids, orders].set(jnp.broadcast_to(jnp.arange(TILES, dtype=jnp.int32)[None, :], (CLIPS, TILES)))
    upper_tile = jnp.take_along_axis(orders, jnp.maximum(position - 1, 0), axis=1)
    upper_tile = jnp.where(position > 0, upper_tile, TILES)
    lower_tile = jnp.take_along_axis(orders, jnp.minimum(position + 1, TILES - 1), axis=1)
    lower_tile = jnp.where(position < TILES - 1, lower_tile, TILES)
    return jnp.stack([upper_tile, lower_tile], axis=-1).astype(jnp.int32)


def draw_rows_used(key, part):
    counts = jax.random.randint(key, (CLIPS, TILES), (ROWS + 3) // 4, ROWS + 1)
    chosen = jax.random.randint(jax.random.fold_in(key, 7), (CLIPS,), 0, TILES)
    tile_ids = jnp.arange(TILES, dtype=jnp.int32)[None, :]
    return jnp.where(tile_ids == chosen[:, None], ROWS, counts).astype(jnp.int32)


def draw_cols_used(key, part):
    counts = jax.random.randint(key, (CLIPS,), COLS // 2, COLS + 1)
    chosen = jax.random.randint(jax.random.fold_in(key, 11), (), 0, CLIPS)
    return jnp.where(jnp.arange(CLIPS, dtype=jnp.int32) == chosen, COLS, counts).astype(jnp.int32)


def steps_of(rng, shape, cuts, low, top_value):
    loudness = 1.0
    for dim, shards_of in cuts:
        heights = jax.random.uniform(jax.random.fold_in(jax.random.fold_in(rng, 6), dim), (shards_of,), jnp.float32, low / len(cuts), top_value / len(cuts))
        loudness = loudness * jnp.repeat(jnp.exp(heights), shape[dim] // shards_of).reshape((-1,) + (1,) * (len(shape) - 1 - dim))
    return loudness


def scatter_about(key, extent, width, limit, shards=(), held_as=jnp.bfloat16):
    values = jax.random.normal(key, extent, jnp.float32) * width
    if len(shards) > 0:
        values = steps_of(key, extent, shards, -0.22, 0.18) * values
    return jnp.clip(values, min=-limit, max=limit).astype(held_as)


def setup_inputs(seed: int = 0) -> dict:
    splits = jax.random.split(jax.random.key(seed), 7)
    video = scatter_about(splits[0], (CLIPS, TILES, FRAMES, ROWS, COLS, CH), 1.0, 6.0, ((0, 4), (1, 4)))
    cotangent = scatter_about(splits[1], (CLIPS, TILES, FRAMES, ROWS, COLS, CH), 1.0, 6.0, ((0, 4), (1, 4)))
    weights = scatter_about(splits[2], (2, 27, CH, CH), (27 * CH) ** -0.5, 0.078125, ((0, 2),))
    neighbours = draw_neighbours(jax.random.fold_in(splits[6], 71), 0)
    rows_used = draw_rows_used(jax.random.fold_in(splits[6], 71), 0)
    cols_used = draw_cols_used(jax.random.fold_in(splits[6], 71), 0)
    return {"video": video, "cotangent": cotangent, "weights": weights, "neighbours": neighbours, "rows_used": rows_used, "cols_used": cols_used}


def silu_grad(values):
    sigmoid = jax.nn.sigmoid(values)
    return sigmoid * (1.0 + values * (1.0 - sigmoid))

def pad_block(strip_field, upper, bottom, row_count):
    frame_count, height, columns, channels = strip_field.shape
    blank = jnp.zeros((frame_count, 1, columns, channels), strip_field.dtype)
    padded = jnp.concatenate([upper[:, None], strip_field, blank], axis=1)
    padded = lax.dynamic_update_slice_in_dim(padded, bottom[:, None], row_count + 1, axis=1)
    return jnp.pad(padded, ((0, 0), (0, 0), (1, 1), (0, 0)))

def patches(stacked, frame_count, height, columns):
    pieces = []
    for depth_off in range(3):
        for row_off in range(3):
            for col_off in range(3):
                pieces.append(stacked[depth_off:depth_off + frame_count, row_off:row_off + height, col_off:col_off + columns])
    return jnp.concatenate(pieces, axis=-1).reshape(frame_count * height * columns, -1)

def last_row(strip_field, row_count):
    return lax.dynamic_index_in_dim(strip_field, row_count - 1, axis=1, keepdims=False)

def one_clip(video, cotangent, weights, neighbours, rows_used, col_count):
    tile_count, frame_count, height, columns, channels = video.shape
    row_ids = jnp.arange(height, dtype=jnp.int32)
    col_ids = jnp.arange(columns, dtype=jnp.int32)
    inside = (row_ids[None, :, None] < rows_used[:, None, None]) & (col_ids[None, None, :] < col_count)
    inside_mask = inside[:, None, :, :, None]
    upper_tile = neighbours[:, 0]
    lower_tile = neighbours[:, 1]

    def halo_all(field):
        leading = field[:, :, 0]
        trailing = jax.vmap(last_row)(field, rows_used)
        upper = trailing[jnp.minimum(upper_tile, tile_count - 1)]
        upper = jnp.where((upper_tile < tile_count)[:, None, None, None], upper, jnp.zeros_like(upper))
        bottom = leading[jnp.minimum(lower_tile, tile_count - 1)]
        bottom = jnp.where((lower_tile < tile_count)[:, None, None, None], bottom, jnp.zeros_like(bottom))
        return jax.vmap(pad_block)(field, upper, bottom, rows_used)

    def tile_patches(stacked):
        return jax.vmap(lambda single: patches(single, frame_count, height, columns))(stacked).reshape(-1, 27 * channels)
    front_zero = jnp.zeros((tile_count, 2, height + 2, columns + 2, channels), jnp.bfloat16)
    forward_mats = [weights[index].reshape(27 * channels, channels) for index in range(2)]
    backward_mat = weights[1][::-1].transpose(0, 2, 1).reshape(27 * channels, channels)
    source = jnp.where(inside_mask, video, jnp.zeros_like(video)).astype(jnp.bfloat16)
    active_zero = jax.nn.silu(source.astype(jnp.float32)).astype(jnp.bfloat16)
    patch_zero = tile_patches(jnp.concatenate([front_zero, halo_all(active_zero)], axis=1))
    mixed = jnp.dot(patch_zero, forward_mats[0], preferred_element_type=jnp.float32).reshape(video.shape)
    hidden = jnp.where(inside_mask, source.astype(jnp.float32) + mixed, 0.0).astype(jnp.bfloat16)
    active_one = jax.nn.silu(hidden.astype(jnp.float32)).astype(jnp.bfloat16)
    patch_one = tile_patches(jnp.concatenate([front_zero, halo_all(active_one)], axis=1))
    mixed = jnp.dot(patch_one, forward_mats[1], preferred_element_type=jnp.float32).reshape(video.shape)
    decoded = jnp.where(inside_mask, hidden.astype(jnp.float32) + mixed, 0.0).astype(jnp.bfloat16)
    target = jnp.where(inside_mask, cotangent, jnp.zeros_like(cotangent)).astype(jnp.bfloat16)
    patch_back = tile_patches(jnp.concatenate([halo_all(target), front_zero], axis=1))
    spread = jnp.dot(patch_back, backward_mat, preferred_element_type=jnp.float32).reshape(video.shape)
    hidden_grad = jnp.where(inside_mask, target.astype(jnp.float32) + silu_grad(hidden.astype(jnp.float32)) * spread, 0.0).astype(jnp.bfloat16)
    grad_zero = jnp.dot(patch_zero.T, hidden_grad.reshape(-1, channels), preferred_element_type=jnp.float32)
    grad_one = jnp.dot(patch_one.T, target.reshape(-1, channels), preferred_element_type=jnp.float32)
    return (jnp.stack([hidden, decoded]), jnp.stack([grad_zero, grad_one]))

def reference(video, cotangent, weights, neighbours, rows_used, cols_used):

    def per_clip(total, inputs):
        clip_video, clip_cot, clip_nbrs, clip_rows, clip_cols = inputs
        outputs, clip_grads = one_clip(clip_video, clip_cot, weights, clip_nbrs, clip_rows, clip_cols)
        return (total + clip_grads, outputs)
    start = jnp.zeros((2, 27 * CH, CH), jnp.float32)
    total, sections = lax.scan(per_clip, start, (video, cotangent, neighbours, rows_used, cols_used))
    section_out = jnp.moveaxis(sections, 0, 1)
    grads = total.reshape(2, 3, 9 * CH * CH)
    return (section_out, grads)
```

```python
import functools

import jax
import jax.numpy as jnp
from jax import lax
from jax.experimental import pallas as pl
from jax.experimental.pallas import tpu as pltpu
from jax.sharding import PartitionSpec as P

MESH = pl.DeviceIdType.MESH
F32, BF16 = jnp.float32, jnp.bfloat16
LEAD = 8


def silu(values):
    return values / (1.0 + jnp.exp(-values))


def silu_grad(values):
    sigmoid = 1.0 / (1.0 + jnp.exp(-values))
    return sigmoid * (1.0 + values * (1.0 - sigmoid))


def share_of(clip, tile, tiles, row_total, channels):
    start = (clip * tiles + tile) * row_total
    return start // channels, start % channels


def block_kernel(
    dims,
    rows_ref,
    cols_ref,
    near_ref,
    video_hbm,
    cot_hbm,
    weight_hbm,
    out_ref,
    grads_ref,
    video,
    cot,
    weight,
    flat,
    wide,
    main_sel,
    rest_sel,
    under_sel,
    taps_mat,
    early_all,
    edge_all,
    late_all,
    halo_one,
    halo_two,
    give,
    got,
    shift_own,
    shift_far,
    result,
    part_send,
    part_recv,
    load_sem,
    early_out,
    edge_out,
    late_out,
    early_in,
    edge_in,
    late_in,
    halo_out,
    halo_in,
    swap_sem,
    part_out,
    part_in,
):
    clips, tiles, frames, height, columns, channels, row_total = dims
    fr = height * columns
    tall = fr + 2 * columns
    rows = frames * fr
    half = channels // 2
    edge_half = columns * (frames + 1)
    section = lax.axis_index("segment")
    clip = lax.axis_index("clip")
    tile = lax.axis_index("tile")
    line = clips == 4
    square = tiles == 4
    inner = (clip + 1) // 2 % 2 == 1

    if line:
        near, over, far = clip + 1 - 2 * (clip % 2), (clip + 2) % 4, 3 - clip
        clip_peers = [over, far, near]
    else:
        clip_peers = [(clip + step) % clips for step in range(1, clips)]
    if square:
        beside, below = tile + 1 - 2 * (tile % 2), (tile + 2) % 4
        tile_peers = [beside, below]
        halo_peers = [beside, below, 3 - tile]
    else:
        tile_peers = halo_peers = [(tile + step) % tiles for step in range(1, tiles)]

    loads = [
        pltpu.make_async_copy(cot_hbm.at[0, 0], cot, load_sem.at[0]),
        pltpu.make_async_copy(video_hbm.at[0, 0], video, load_sem.at[1]),
        pltpu.make_async_copy(weight_hbm.at[0], weight, load_sem.at[2]),
    ]
    for load in loads:
        load.start()

    twin = (1 - section, clip, tile)
    barrier = pltpu.get_barrier_semaphore()
    greeted = [twin]
    greeted += [(section, peer, tile) for peer in clip_peers]
    greeted += [(section, clip, peer) for peer in halo_peers]
    for place in greeted:
        pl.semaphore_signal(barrier, inc=1, device_id=place, device_id_type=MESH)

    row_count = rows_ref[0, 0]
    col_count = cols_ref[0]
    upper_tile = near_ref[0, 0, 0]
    lower_tile = near_ref[0, 0, 1]
    ids = lax.broadcasted_iota(jnp.int32, (fr, channels), 0)
    column = ids % columns
    row_id = ids // columns
    inside = (row_id < row_count) & (column < col_count)

    started = []

    def transfer(ref, slot, send_sem, recv_sem, place):
        return pltpu.make_async_remote_copy(
            src_ref=ref.at[slot],
            dst_ref=ref.at[slot],
            send_sem=send_sem,
            recv_sem=recv_sem,
            device_id=place,
            device_id_type=MESH,
        )

    def go(copy, only=None):
        started.append((copy, only))
        if only is None:
            copy.start()
        else:
            pl.when(only)(copy.start)

    class Field:
        def __init__(self, ref, outs, ins):
            self.ref, self.outs, self.ins, self.used = ref, outs, ins, 0

        def send(self, slot_clip, place, only=None):
            copy = transfer(
                self.ref,
                (slot_clip, tile),
                self.outs.at[self.used],
                self.ins.at[slot_clip, tile],
                place,
            )
            self.used += 1
            go(copy, only)

        def send_own(self):
            for peer in clip_peers:
                skip = line and peer is far
                self.send(clip, (section, peer, tile), inner if skip else None)
            for peer in tile_peers:
                self.send(clip, (section, clip, peer))

        def arrived(self, slot_clip, slot_tile):
            transfer(
                self.ref,
                (slot_clip, slot_tile),
                self.outs.at[0],
                self.ins.at[slot_clip, slot_tile],
                twin,
            ).wait_recv()

        def along(self):
            self.send(over, (section, near, tile), inner)

        def across(self, slot_clip):
            for peer in tile_peers:
                self.send(slot_clip, (section, clip, peer))

    early = Field(early_all, early_out, early_in)
    edge = Field(edge_all, edge_out, edge_in)
    late = Field(late_all, late_out, late_in)

    def read_field(source, target):
        for frame in range(frames):
            for row in range(height):
                low = fr * frame + columns * row
                target[low : low + columns] = source[frame, row].astype(F32)

    def frame_of(ref, frame):
        return ref[fr * frame : fr * (frame + 1)]

    def ends_of(ref):
        leading = [ref[fr * f : fr * f + columns] for f in range(frames)]
        trailing = []
        for f in range(frames):
            last = leading[f]
            for row in range(1, height):
                low = fr * f + columns * row
                last = jnp.where(row_count - 1 == row, ref[low : low + columns], last)
            trailing.append(last)
        blank = jnp.zeros((columns, channels), F32)
        return jnp.concatenate(leading + [blank] + trailing + [blank], axis=0)

    def send_halo(ref, number):
        for index, peer in enumerate(halo_peers):
            copy = transfer(
                ref,
                tile,
                halo_out.at[number, index],
                halo_in.at[number, tile],
                (section, clip, peer),
            )
            go(copy)

    def take_halo(ref, number):
        for peer in halo_peers:
            transfer(ref, peer, halo_out.at[number, 0], halo_in.at[number, peer], twin).wait_recv()
        above = ref[jnp.minimum(upper_tile, tiles - 1)].astype(F32)
        under = ref[jnp.minimum(lower_tile, tiles - 1)].astype(F32)
        above = jnp.where(upper_tile < tiles, above[edge_half : 2 * edge_half], 0.0)
        under = jnp.where(lower_tile < tiles, under[:edge_half], 0.0)
        return above, under

    def repeated(block, count):
        return jnp.concatenate([block] * count, axis=0)

    def write_frame(target, frame, main, top, bottom, hit, full):
        base = LEAD + tall * frame
        target[base : base + columns] = top
        target[base + columns : base + columns + fr] = jnp.where(
            hit, repeated(bottom, height), main
        )
        target[base + columns + fr : base + tall] = jnp.where(full, bottom, 0.0)

    def pad_own(above, under):
        hit = row_id == row_count
        full = row_count == height
        for f in range(frames):
            low = columns * f
            write_frame(
                wide,
                f,
                frame_of(flat, f),
                above[low : low + columns],
                under[low : low + columns],
                hit,
                full,
            )

    def make_taps():
        for f in range(frames):
            for row_off in range(3):
                for col_off in range(3):
                    start = LEAD + tall * f + columns * row_off + col_off - 1
                    block = wide[start : start + fr]
                    if col_off == 0:
                        block = jnp.where(column > 0, block, 0.0)
                    if col_off == 2:
                        block = jnp.where(column < columns - 1, block, 0.0)
                    taps_mat[
                        row_off,
                        fr * f : fr * (f + 1),
                        channels * col_off : channels * (col_off + 1),
                    ] = block.astype(BF16)

    def conv_front():
        sums = [jnp.zeros((fr, channels), F32) for _ in range(frames)]
        for depth_off in range(3):
            count = frames - 2 + depth_off
            part = jnp.zeros((fr * count, channels), F32)
            for row_off in range(3):
                tap = 9 * depth_off + 3 * row_off
                part += jnp.dot(
                    taps_mat[row_off, : fr * count, :],
                    weight[tap : tap + 3].reshape(3 * channels, channels),
                    preferred_element_type=F32,
                )
            for n in range(count):
                sums[frames - count + n] += part[fr * n : fr * (n + 1)]
        return sums

    def conv_back():
        sums = [jnp.zeros((fr, channels), F32) for _ in range(frames)]
        for depth_off in range(3):
            count = frames - depth_off
            part = jnp.zeros((fr * count, channels), F32)
            for row_off in range(3):
                for col_off in range(3):
                    tap = 9 * depth_off + 3 * row_off + col_off
                    part += lax.dot_general(
                        taps_mat[
                            row_off,
                            fr * depth_off :,
                            channels * col_off : channels * (col_off + 1),
                        ],
                        weight[26 - tap],
                        (((1,), (1,)), ((), ())),
                        preferred_element_type=F32,
                    )
            for n in range(count):
                sums[n] += part[fr * n : fr * (n + 1)]
        return sums

    def write_out(frame, values):
        for row in range(height):
            out_ref[frame, row] = values[columns * row : columns * (row + 1)].astype(BF16)

    def shares(dest_tile):
        tap, first = share_of(clip, dest_tile, tiles, row_total, channels)
        return tap, jnp.minimum(tap + 1, 8), first

    dests = [tile] + (tile_peers if square else [])

    def make_selections():
        place = lax.broadcasted_iota(jnp.int32, (rows, 128), 0)
        lane = lax.broadcasted_iota(jnp.int32, (rows, 128), 1)
        col_id = place % columns
        line_id = place // columns
        frame_id = line_id // height
        line_id = line_id - height * frame_id
        for dest, dest_tile in enumerate(dests):
            for half_id, tap in enumerate(shares(dest_tile)[:2]):
                row_off, col_off = tap // 3, tap % 3
                row_off = row_off + section * (2 - 2 * row_off) - 1
                col_off = col_off + section * (2 - 2 * col_off) - 1
                there, beyond = line_id + row_off, col_id + col_off
                valid = (beyond >= 0) & (beyond < columns)
                main = jnp.where(
                    valid & (there >= 0) & (there < height),
                    place + columns * row_off + col_off,
                    -1,
                )
                rim = jnp.where(valid, columns * frame_id + beyond, -4 * rows)
                top = jnp.where(there == -1, rim + rows, -1)
                low = rows * half_id
                main_sel[dest, low : low + rows] = jnp.where(lane == main, 1.0, 0.0).astype(BF16)
                rest = (lane + 128 == main) | (lane + 128 == top)
                rest_sel[dest, low : low + rows] = jnp.where(rest, 1.0, 0.0)
                under_sel[dest, low : low + rows] = jnp.where(
                    lane + 128 == rim + rows + edge_half, there.astype(F32), -5.0
                )

    is_encoder = section == 0
    is_decoder = section != 0
    wide[...] = jnp.zeros(wide.shape, F32)
    loads[0].wait()
    loads[1].wait()

    @pl.when(is_encoder)
    def _():
        read_field(video, flat)
        for f in range(frames):
            values = jnp.where(inside, frame_of(flat, f), 0.0)
            active = silu(values).astype(BF16)
            early_all[clip, tile, fr * f : fr * (f + 1)] = active
            flat[fr * f : fr * (f + 1)] = active.astype(F32)

    @pl.when(is_decoder)
    def _():
        read_field(cot, flat)
        for f in range(frames):
            values = jnp.where(inside, frame_of(flat, f), 0.0)
            early_all[clip, tile, fr * f : fr * (f + 1)] = values.astype(BF16)
            flat[fr * f : fr * (f + 1)] = values

    halo_one[tile] = ends_of(flat).astype(BF16)
    pl.semaphore_wait(barrier, len(greeted))
    send_halo(halo_one, 0)
    early.send_own()
    make_selections()

    above, under = take_halo(halo_one, 0)
    pad_own(above, under)
    count_rows = jnp.zeros((columns, channels), F32) + row_count.astype(F32)
    edge_all[clip, tile] = jnp.concatenate(
        [above[: edge_half - columns], count_rows, under], axis=0
    ).astype(BF16)
    edge.send_own()
    make_taps()
    loads[2].wait()

    @pl.when(is_encoder)
    def _():
        read_field(video, flat)
        sums = conv_front()
        for f in range(frames):
            values = jnp.where(inside, frame_of(flat, f) + sums[f], 0.0).astype(BF16)
            give[fr * f : fr * (f + 1)] = values.astype(F32)

    @pl.when(is_decoder)
    def _():
        sums = conv_back()
        for f in range(frames):
            give[fr * f : fr * (f + 1)] = sums[f]

    swap = pltpu.make_async_remote_copy(
        src_ref=give,
        dst_ref=got,
        send_sem=swap_sem.at[0],
        recv_sem=swap_sem.at[1],
        device_id=twin,
        device_id_type=MESH,
    )
    go(swap)

    @pl.when(is_encoder)
    def _():
        read_field(cot, flat)
        for f in range(frames):
            write_out(f, frame_of(give, f))

    if line:
        early.arrived(over, tile)
        early.along()
    swap.wait_recv()

    @pl.when(is_encoder)
    def _():
        for f in range(frames):
            target = frame_of(flat, f)
            values = target + silu_grad(frame_of(give, f)) * frame_of(got, f)
            late_all[clip, tile, fr * f : fr * (f + 1)] = jnp.where(inside, values, 0.0).astype(
                BF16
            )

    @pl.when(is_decoder)
    def _():
        for f in range(frames):
            active = silu(frame_of(got, f)).astype(BF16)
            late_all[clip, tile, fr * f : fr * (f + 1)] = active
            flat[fr * f : fr * (f + 1)] = active.astype(F32)
        halo_two[tile] = ends_of(flat).astype(BF16)

    late.send_own()
    send_halo(halo_two, 1)
    if line:
        edge.arrived(over, tile)
        edge.along()

    for peer in reversed(clip_peers):
        if not (line and peer is over):
            early.arrived(peer, tile)
        early.across(peer)
    for peer in reversed(clip_peers):
        if not (line and peer is over):
            edge.arrived(peer, tile)
        edge.across(peer)

    above, under = take_halo(halo_two, 1)

    @pl.when(is_decoder)
    def _():
        pad_own(above, under)
        make_taps()
        sums = conv_front()
        for f in range(frames):
            write_out(f, jnp.where(inside, frame_of(got, f) + sums[f], 0.0))

    def make_shift(target, slot, source_tile, dest):
        first = shares(dests[dest])[2]
        lane = lax.broadcasted_iota(jnp.int32, (rows, channels), 1)
        keep_first = (lane >= first) | is_decoder

        @pl.loop(0, clips)
        def _(index):
            rim = edge_all[index, source_tile]
            count = rim.astype(F32)[edge_half - columns : edge_half - columns + 1, :128]
            rest = rest_sel[dest] + jnp.where(under_sel[dest] == count, 1.0, 0.0)
            picks = jnp.concatenate([main_sel[dest], rest.astype(BF16)], axis=1)
            field = jnp.concatenate([early_all[index, source_tile], rim], axis=0)
            moved = jnp.dot(
                picks[:, : rows + 2 * edge_half], field, preferred_element_type=F32
            )
            picked = jnp.where(keep_first, moved[:rows], moved[rows:])
            target[slot, index, :, :channels] = picked.astype(BF16)
            target[slot, index, :, channels:] = moved[rows:].astype(BF16)

    def column_arrived(field, source_tile):
        for index in range(clips):
            field.arrived(index, source_tile)

    make_shift(shift_own, 0, tile, 0)
    clip_order = reversed(clip_peers) if not line else [over, near, far]
    for peer in clip_order:
        late.arrived(peer, tile)
        if line and peer is over:
            late.along()
        late.across(peer)
    for number, peer in enumerate(tile_peers):
        column_arrived(early, peer)
        column_arrived(edge, peer)
        make_shift(shift_own, number + 1, peer, 0)
        if square:
            make_shift(shift_far, number, peer, 2 - number)

    def stacked(ref, lead, low, count, lanes):
        blocks = [
            ref[lead(index) + (slice(fr * low, fr * (low + count)), lanes)]
            for index in range(clips)
        ]
        return jnp.concatenate(blocks, axis=0)

    contract = (((0,), (0,)), ((), ()))
    whole = slice(0, channels)

    def products(shift, slot, source_tile, dest_tile, tap, side):
        count = frames - 2 + tap
        _, _, first = shares(dest_tile)
        shift_at = lambda index: (slot, index)
        late_at = lambda index: (index, source_tile)
        lanes = whole if side is None else slice(half * side, half * (side + 1))
        width = lanes.stop - lanes.start
        if_encoder = lambda: lax.dot_general(
            stacked(shift, shift_at, 0, count, whole),
            stacked(late_all, late_at, frames - count, count, lanes),
            contract,
            preferred_element_type=F32,
        )

        def if_decoder():
            acts = stacked(late_all, late_at, 0, count, whole)
            sums = [
                lax.dot_general(
                    acts,
                    stacked(
                        shift,
                        shift_at,
                        frames - count,
                        count,
                        slice(base + lanes.start, base + lanes.stop),
                    ),
                    contract,
                    preferred_element_type=F32,
                )
                for base in (0, channels)
            ]
            rows = lax.broadcasted_iota(jnp.int32, (channels, width), 0)
            return jnp.where(rows >= first, sums[0], sums[1])

        return if_encoder, if_decoder

    def keep(tap, width, values):
        result[tap, :channels, :width] = values
        result[tap, channels : 2 * channels, :width] = values

    def window(tap, dest_tile, width):
        _, _, first = shares(dest_tile)
        if row_total % 16 == 0:
            first = pl.multiple_of(first, 16)
            return result[tap, pl.ds(first, row_total), :width]
        turned = pltpu.roll(result[tap, :channels, :width], (channels - first) % channels, 0)
        return turned[:row_total]

    if square:
        for number, peer in enumerate(tile_peers):
            dest = tile_peers[1 - number]
            column_arrived(late, peer)
            for tap in range(3):
                for_encoder, for_decoder = products(shift_far, number, peer, dest, tap, number)
                pl.when(is_encoder)(lambda: keep(tap, half, for_encoder()))
                pl.when(is_decoder)(lambda: keep(tap, half, for_decoder()))
                part_send[number, tap] = window(tap, dest, half).astype(BF16)
            go(
                pltpu.make_async_remote_copy(
                    src_ref=part_send.at[number],
                    dst_ref=part_recv.at[number],
                    send_sem=part_out.at[number],
                    recv_sem=part_in.at[number],
                    device_id=(section, clip, dest),
                    device_id_type=MESH,
                )
            )
    else:
        for peer in tile_peers:
            column_arrived(late, peer)

    for tap in range(3):
        if square:
            sources = [tile] + tile_peers
            for which, chosen in ((0, is_encoder), (1, is_decoder)):

                @pl.when(chosen)
                def _():
                    total = None
                    for slot, source in enumerate(sources):
                        part = products(shift_own, slot, source, tile, tap, None)[which]()
                        total = part if total is None else total + part
                    keep(tap, channels, total)

        else:
            result[tap, :channels] = jnp.zeros((channels, channels), F32)
            for which, chosen in ((0, is_encoder), (1, is_decoder)):

                @pl.when(chosen)
                def _():
                    @pl.loop(0, tiles)
                    def _(slot):
                        source = (tile + slot) % tiles
                        result[tap, :channels] += products(
                            shift_own, slot, source, tile, tap, None
                        )[which]()

            result[tap, channels : 2 * channels] = result[tap, :channels]

    if square:
        for number in range(2):
            pltpu.make_async_remote_copy(
                src_ref=part_recv.at[number],
                dst_ref=part_recv.at[number],
                send_sem=part_out.at[number],
                recv_sem=part_in.at[number],
                device_id=twin,
                device_id_type=MESH,
            ).wait_recv()
    for tap in range(3):
        own = window(tap, tile, channels)
        if square:
            own += jnp.concatenate(
                [part_recv[0, tap].astype(F32), part_recv[1, tap].astype(F32)], axis=1
            )
        grads_ref[tap] = own

    for copy, only in started:
        if only is None:
            copy.wait_send()
        else:
            pl.when(only)(copy.wait_send)


def local(video, cotangent, weights, neighbours, rows_used, cols_used):
    frames, height, columns, channels = video.shape[2:]
    clips, tiles = lax.axis_size("clip"), lax.axis_size("tile")
    row_total = 9 * channels // (clips * tiles)
    rows = frames * height * columns
    dims = (clips, tiles, frames, height, columns, channels, row_total)
    edge_rows = 2 * columns * (frames + 1)
    padded = 2 * LEAD + frames * (height + 2) * columns
    peers = 2 if tiles == 4 else tiles - 1
    count = (clips - 1 + (1 if clips == 4 else 0)) + peers + (clips - 1) * peers
    dma = pltpu.SemaphoreType.DMA
    own_out, summed = pl.pallas_call(
        functools.partial(block_kernel, dims),
        out_shape=(
            jax.ShapeDtypeStruct((frames, height, columns, channels), BF16),
            jax.ShapeDtypeStruct((3, row_total, channels), F32),
        ),
        in_specs=[pl.BlockSpec(memory_space=pltpu.SMEM)] * 3 + [pl.BlockSpec(memory_space=pl.ANY)] * 3,
        out_specs=(pl.BlockSpec(memory_space=pltpu.VMEM),) * 2,
        scratch_shapes=[
            pltpu.VMEM((frames, height, columns, channels), BF16),
            pltpu.VMEM((frames, height, columns, channels), BF16),
            pltpu.VMEM((27, channels, channels), BF16),
            pltpu.VMEM((rows, channels), F32),
            pltpu.VMEM((padded, channels), F32),
            pltpu.VMEM((3, 2 * rows, 128), BF16),
            pltpu.VMEM((3, 2 * rows, 128), F32),
            pltpu.VMEM((3, 2 * rows, 128), F32),
            pltpu.VMEM((3, rows, 3 * channels), BF16),
            pltpu.VMEM((clips, tiles, rows, channels), BF16),
            pltpu.VMEM((clips, tiles, edge_rows, channels), BF16),
            pltpu.VMEM((clips, tiles, rows, channels), BF16),
            pltpu.VMEM((tiles, edge_rows, channels), BF16),
            pltpu.VMEM((tiles, edge_rows, channels), BF16),
            pltpu.VMEM((rows, channels), F32),
            pltpu.VMEM((rows, channels), F32),
            pltpu.VMEM((peers + 1, clips, rows, 2 * channels), BF16),
            pltpu.VMEM((2, clips, rows, 2 * channels), BF16),
            pltpu.VMEM((3, 2 * channels, channels), F32),
            pltpu.VMEM((2, 3, row_total, channels // 2), BF16),
            pltpu.VMEM((2, 3, row_total, channels // 2), BF16),
            dma((3,)),
            dma((count,)),
            dma((count,)),
            dma((count,)),
            dma((clips, tiles)),
            dma((clips, tiles)),
            dma((clips, tiles)),
            dma((2, tiles - 1)),
            dma((2, tiles)),
            dma((2,)),
            dma((2,)),
            dma((2,)),
        ],
        compiler_params=pltpu.CompilerParams(
            collective_id=0, has_side_effects=True, vmem_limit_bytes=56 * 2**20
        ),
    )(rows_used, cols_used, neighbours, video, cotangent, weights)
    return (own_out[None, None, None], summed.reshape(1, 3, row_total * channels))


def solution(mesh):
    in_specs = (
        P("clip", "tile", None, None, None, None),
        P("clip", "tile", None, None, None, None),
        P("segment", None, None, None),
        P("clip", "tile", None),
        P("clip", "tile"),
        P("clip"),
    )
    out_specs = (
        P("segment", "clip", "tile", None, None, None, None),
        P("segment", None, ("clip", "tile")),
    )
    return jax.shard_map(local, mesh=mesh, in_specs=in_specs, out_specs=out_specs, check_vma=False)
```

```python
import functools

import jax
import jax.numpy as jnp
from jax import lax
from jax.experimental import pallas as pl
from jax.experimental.pallas import tpu as pltpu
from jax.sharding import PartitionSpec as P

MESH = pl.DeviceIdType.MESH
F32, BF16 = jnp.float32, jnp.bfloat16
LEAD = 8


def silu(values):
    return values / (1.0 + jnp.exp(-values))


def silu_grad(values):
    sigmoid = 1.0 / (1.0 + jnp.exp(-values))
    return sigmoid * (1.0 + values * (1.0 - sigmoid))


def share_of(clip, tile, tiles, row_total, channels):
    start = (clip * tiles + tile) * row_total
    return start // channels, start % channels


def block_kernel(
    dims,
    rows_ref,
    cols_ref,
    near_hbm,
    video_hbm,
    cot_hbm,
    weight_hbm,
    out_ref,
    grads_ref,
    near_ref,
    video,
    cot,
    weight,
    flat,
    wide,
    main_sel,
    rest_sel,
    under_sel,
    taps_mat,
    early_all,
    edge_all,
    late_all,
    halo_one,
    halo_two,
    give,
    got,
    shift_own,
    shift_far,
    result,
    part_send,
    part_recv,
    rows_send,
    rows_recv,
    load_sem,
    early_out,
    edge_out,
    late_out,
    early_in,
    edge_in,
    late_in,
    halo_out,
    halo_in,
    swap_sem,
    part_out,
    part_in,
):
    clips, tiles, frames, height, columns, channels, row_total = dims
    fr = height * columns
    tall = fr + 2 * columns
    rows = frames * fr
    half = channels // 2
    edge_half = columns * (frames + 1)
    section = lax.axis_index("segment")
    clip = lax.axis_index("clip")
    tile = lax.axis_index("tile")
    line = clips == 4
    square = tiles == 4
    inner = (clip + 1) // 2 % 2 == 1

    if line:
        near, over, far = clip + 1 - 2 * (clip % 2), (clip + 2) % 4, 3 - clip
        clip_peers = [over, far, near]
    else:
        clip_peers = [(clip + step) % clips for step in range(1, clips)]
    if square:
        beside, below = tile + 1 - 2 * (tile % 2), (tile + 2) % 4
        tile_peers = [beside, below]
        halo_peers = [beside, below, 3 - tile]
    else:
        tile_peers = halo_peers = [(tile + step) % tiles for step in range(1, tiles)]

    loads = [
        pltpu.make_async_copy(cot_hbm.at[0, 0], cot, load_sem.at[0]),
        pltpu.make_async_copy(video_hbm.at[0, 0], video, load_sem.at[1]),
        pltpu.make_async_copy(weight_hbm.at[0], weight, load_sem.at[2]),
        pltpu.make_async_copy(near_hbm, near_ref, load_sem.at[3]),
    ]
    for index in (0, 1, 3, 2):
        loads[index].start()

    twin = (1 - section, clip, tile)
    barrier = pltpu.get_barrier_semaphore()
    greeted = [twin]
    greeted += [(section, peer, tile) for peer in clip_peers]
    greeted += [(section, clip, peer) for peer in halo_peers]
    for place in greeted:
        pl.semaphore_signal(barrier, inc=1, device_id=place, device_id_type=MESH)

    row_count = jnp.broadcast_to(rows_ref[...], (fr, channels))
    col_count = jnp.broadcast_to(cols_ref[...], (fr, channels))
    ids = lax.broadcasted_iota(jnp.int32, (fr, channels), 0)
    column = ids % columns
    row_id = ids // columns
    inside = (row_id < row_count) & (column < col_count)

    started = []

    def transfer(ref, slot, send_sem, recv_sem, place):
        return pltpu.make_async_remote_copy(
            src_ref=ref.at[slot],
            dst_ref=ref.at[slot],
            send_sem=send_sem,
            recv_sem=recv_sem,
            device_id=place,
            device_id_type=MESH,
        )

    def go(copy, only=None):
        started.append((copy, only))
        if only is None:
            copy.start()
        else:
            pl.when(only)(copy.start)

    class Field:
        def __init__(self, ref, outs, ins, halved=False):
            self.ref, self.outs, self.ins, self.used = ref, outs, ins, 0
            self.halved = halved

        def part(self, slot_clip, slot_tile, side):
            if side is None:
                return slot_clip, slot_tile
            return slot_clip, slot_tile, slice(None), pl.ds(half * side, half)

        def send(self, slot_clip, place, only=None, side=None):
            copy = transfer(
                self.ref,
                self.part(slot_clip, tile, side),
                self.outs.at[self.used],
                self.ins.at[slot_clip, tile],
                place,
            )
            self.used += 1
            go(copy, only)

        def send_own(self):
            for peer in clip_peers:
                skip = line and peer is far
                self.send(clip, (section, peer, tile), inner if skip else None)
            self.across(clip)

        def arrived(self, slot_clip, slot_tile, side=None):
            transfer(
                self.ref,
                self.part(slot_clip, slot_tile, side),
                self.outs.at[0],
                self.ins.at[slot_clip, slot_tile],
                twin,
            ).wait_recv()

        def along(self):
            self.send(over, (section, near, tile), inner)

        def across(self, slot_clip):
            for number, peer in enumerate(tile_peers):
                side = number if self.halved else None
                self.send(slot_clip, (section, clip, peer), None, side)

    early = Field(early_all, early_out, early_in)
    edge = Field(edge_all, edge_out, edge_in)
    late = Field(late_all, late_out, late_in, square)

    def read_field(source, target):
        for frame in range(frames):
            for row in range(height):
                low = fr * frame + columns * row
                target[low : low + columns] = source[frame, row].astype(F32)

    def frame_of(ref, frame):
        return ref[fr * frame : fr * (frame + 1)]

    def ends_of(ref):
        leading = [ref[fr * f : fr * f + columns] for f in range(frames)]
        trailing = []
        for f in range(frames):
            last = leading[f]
            for row in range(1, height):
                low = fr * f + columns * row
                last = jnp.where(row_count[:columns] == row + 1, ref[low : low + columns], last)
            trailing.append(last)
        blank = jnp.zeros((columns, channels), F32)
        return jnp.concatenate(leading + [blank] + trailing + [blank], axis=0)

    def send_halo(ref, number, only=None):
        for index, peer in enumerate(halo_peers):
            copy = transfer(
                ref,
                tile,
                halo_out.at[number, index],
                halo_in.at[number, tile],
                (section, clip, peer),
            )
            go(copy, only)

    def take_halo(ref, number):
        for peer in halo_peers:
            transfer(ref, peer, halo_out.at[number, 0], halo_in.at[number, peer], twin).wait_recv()
        upper_tile = near_ref[0, 0, 0]
        lower_tile = near_ref[0, 0, 1]
        above = ref[jnp.minimum(upper_tile, tiles - 1)].astype(F32)
        under = ref[jnp.minimum(lower_tile, tiles - 1)].astype(F32)
        above = jnp.where(upper_tile < tiles, above[edge_half : 2 * edge_half], 0.0)
        under = jnp.where(lower_tile < tiles, under[:edge_half], 0.0)
        return above, under

    def repeated(block, count):
        return jnp.concatenate([block] * count, axis=0)

    def write_frame(target, frame, main, top, bottom, hit, full):
        base = LEAD + tall * frame
        target[base : base + columns] = top
        target[base + columns : base + columns + fr] = jnp.where(
            hit, repeated(bottom, height), main
        )
        target[base + columns + fr : base + tall] = jnp.where(full, bottom, 0.0)

    def pad_own(above, under):
        hit = row_id == row_count
        full = row_count[:columns] == height
        for f in range(frames):
            low = columns * f
            write_frame(
                wide,
                f,
                frame_of(flat, f),
                above[low : low + columns],
                under[low : low + columns],
                hit,
                full,
            )

    def make_taps():
        for f in range(frames):
            for row_off in range(3):
                for col_off in range(3):
                    start = LEAD + tall * f + columns * row_off + col_off - 1
                    block = wide[start : start + fr]
                    if col_off == 0:
                        block = jnp.where(column > 0, block, 0.0)
                    if col_off == 2:
                        block = jnp.where(column < columns - 1, block, 0.0)
                    taps_mat[
                        row_off,
                        fr * f : fr * (f + 1),
                        channels * col_off : channels * (col_off + 1),
                    ] = block.astype(BF16)

    def conv_front():
        sums = [jnp.zeros((fr, channels), F32) for _ in range(frames)]
        for depth_off in range(3):
            count = frames - 2 + depth_off
            part = jnp.zeros((fr * count, channels), F32)
            for row_off in range(3):
                tap = 9 * depth_off + 3 * row_off
                part += jnp.dot(
                    taps_mat[row_off, : fr * count, :],
                    weight[tap : tap + 3].reshape(3 * channels, channels),
                    preferred_element_type=F32,
                )
            for n in range(count):
                sums[frames - count + n] += part[fr * n : fr * (n + 1)]
        return sums

    def conv_back():
        sums = [jnp.zeros((fr, channels), F32) for _ in range(frames)]
        for depth_off in range(3):
            count = frames - depth_off
            part = jnp.zeros((fr * count, channels), F32)
            for row_off in range(3):
                for col_off in range(3):
                    tap = 9 * depth_off + 3 * row_off + col_off
                    part += lax.dot_general(
                        taps_mat[
                            row_off,
                            fr * depth_off :,
                            channels * col_off : channels * (col_off + 1),
                        ],
                        weight[26 - tap],
                        (((1,), (1,)), ((), ())),
                        preferred_element_type=F32,
                    )
            for n in range(count):
                sums[n] += part[fr * n : fr * (n + 1)]
        return sums

    def write_out(frame, values):
        for row in range(height):
            out_ref[frame, row] = values[columns * row : columns * (row + 1)].astype(BF16)

    def shares(dest_tile):
        tap, first = share_of(clip, dest_tile, tiles, row_total, channels)
        return tap, jnp.minimum(tap + 1, 8), first

    dests = [tile] + (tile_peers if square else [])

    def make_selections():
        place = lax.broadcasted_iota(jnp.int32, (rows, 128), 0)
        lane = lax.broadcasted_iota(jnp.int32, (rows, 128), 1)
        col_id = place % columns
        line_id = place // columns
        frame_id = line_id // height
        line_id = line_id - height * frame_id
        for dest, dest_tile in enumerate(dests):
            for half_id, tap in enumerate(shares(dest_tile)[:2]):
                row_off, col_off = tap // 3, tap % 3
                row_off = row_off + section * (2 - 2 * row_off) - 1
                col_off = col_off + section * (2 - 2 * col_off) - 1
                there, beyond = line_id + row_off, col_id + col_off
                valid = (beyond >= 0) & (beyond < columns)
                main = jnp.where(
                    valid & (there >= 0) & (there < height),
                    place + columns * row_off + col_off,
                    -1,
                )
                rim = jnp.where(valid, columns * frame_id + beyond, -4 * rows)
                top = jnp.where(there == -1, rim + rows, -1)
                low = rows * half_id
                main_sel[dest, low : low + rows] = jnp.where(lane == main, 1.0, 0.0).astype(BF16)
                rest = (lane + 128 == main) | (lane + 128 == top)
                rest_sel[dest, low : low + rows] = jnp.where(rest, 1.0, 0.0)
                under_sel[dest, low : low + rows] = jnp.where(
                    lane + 128 == rim + rows + edge_half, there.astype(F32), -5.0
                )

    is_encoder = section == 0
    is_decoder = section != 0
    wide[...] = jnp.zeros(wide.shape, F32)
    loads[0].wait()
    loads[1].wait()

    @pl.when(is_encoder)
    def _():
        read_field(video, flat)
        for f in range(frames):
            values = jnp.where(inside, frame_of(flat, f), 0.0)
            active = silu(values).astype(BF16)
            early_all[clip, tile, fr * f : fr * (f + 1)] = active
            flat[fr * f : fr * (f + 1)] = active.astype(F32)

    @pl.when(is_decoder)
    def _():
        read_field(cot, flat)
        for f in range(frames):
            values = jnp.where(inside, frame_of(flat, f), 0.0)
            early_all[clip, tile, fr * f : fr * (f + 1)] = values.astype(BF16)
            flat[fr * f : fr * (f + 1)] = values

    halo_one[tile] = ends_of(flat).astype(BF16)
    pl.semaphore_wait(barrier, len(greeted))
    send_halo(halo_one, 0)
    early.send_own()
    make_selections()

    loads[3].wait()
    above, under = take_halo(halo_one, 0)
    pad_own(above, under)
    count_rows = row_count[:columns].astype(F32)
    edge_all[clip, tile] = jnp.concatenate(
        [above[: edge_half - columns], count_rows, under], axis=0
    ).astype(BF16)
    edge.send_own()
    make_taps()
    loads[2].wait()

    @pl.when(is_encoder)
    def _():
        read_field(video, flat)
        sums = conv_front()
        for f in range(frames):
            values = jnp.where(inside, frame_of(flat, f) + sums[f], 0.0).astype(BF16)
            give[fr * f : fr * (f + 1)] = values.astype(F32)

    @pl.when(is_decoder)
    def _():
        sums = conv_back()
        for f in range(frames):
            give[fr * f : fr * (f + 1)] = sums[f]

    swap = pltpu.make_async_remote_copy(
        src_ref=give,
        dst_ref=got,
        send_sem=swap_sem.at[0],
        recv_sem=swap_sem.at[1],
        device_id=twin,
        device_id_type=MESH,
    )
    go(swap)

    @pl.when(is_encoder)
    def _():
        read_field(cot, flat)
        for f in range(frames):
            write_out(f, frame_of(give, f))

    if line:
        early.arrived(over, tile)
        early.along()
        early.across(over)
        early.arrived(near, tile)
        early.across(near)
    swap.wait_recv()

    @pl.when(is_encoder)
    def _():
        for f in range(frames):
            target = frame_of(flat, f)
            values = target + silu_grad(frame_of(give, f)) * frame_of(got, f)
            late_all[clip, tile, fr * f : fr * (f + 1)] = jnp.where(inside, values, 0.0).astype(
                BF16
            )

    @pl.when(is_decoder)
    def _():
        for f in range(frames):
            active = silu(frame_of(got, f)).astype(BF16)
            late_all[clip, tile, fr * f : fr * (f + 1)] = active
            flat[fr * f : fr * (f + 1)] = active.astype(F32)
        halo_two[tile] = ends_of(flat).astype(BF16)

    def make_shift(target, slot, source_tile, dest):
        first = shares(dests[dest])[2]
        lane = lax.broadcasted_iota(jnp.int32, (rows, channels), 1)
        keep_first = (lane >= first) | is_decoder

        @pl.loop(0, clips, unroll=clips if square else 1)
        def _(index):
            rim = edge_all[index, source_tile]
            count = rim.astype(F32)[edge_half - columns : edge_half - columns + 1, :128]
            rest = rest_sel[dest] + jnp.where(under_sel[dest] == count, 1.0, 0.0)
            picks = jnp.concatenate([main_sel[dest], rest.astype(BF16)], axis=1)
            field = jnp.concatenate([early_all[index, source_tile], rim], axis=0)
            moved = jnp.dot(
                picks[:, : rows + 2 * edge_half], field, preferred_element_type=F32
            )
            picked = jnp.where(keep_first, moved[:rows], moved[rows:])
            target[slot, index, :, :channels] = picked.astype(BF16)
            target[slot, index, :, channels:] = moved[rows:].astype(BF16)

    def column_arrived(field, source_tile, side=None):
        for index in range(clips):
            field.arrived(index, source_tile, side)

    def shift_column(number):
        peer = tile_peers[number]
        column_arrived(early, peer)
        column_arrived(edge, peer)
        make_shift(shift_far, 2 * number + 1, peer, 2 - number)
        make_shift(shift_own, number + 1, peer, 0)

    late.send_own()
    send_halo(halo_two, 1, is_decoder)
    if line:
        edge.arrived(over, tile)
        edge.along()

    for peer in [far] if line else clip_peers:
        early.arrived(peer, tile)
        early.across(peer)
    for peer in reversed(clip_peers):
        if not (line and peer is over):
            edge.arrived(peer, tile)
        edge.across(peer)

    make_shift(shift_own, 0, tile, 0)
    if square:
        for number in range(2):
            make_shift(shift_far, 2 * number, tile, 2 - number)
    for peer in [over, near] if line else clip_peers:
        late.arrived(peer, tile)
        if line and peer is over:
            late.along()
        late.across(peer)

    @pl.when(is_decoder)
    def _():
        pad_own(*take_halo(halo_two, 1))
        make_taps()
        sums = conv_front()
        for f in range(frames):
            write_out(f, jnp.where(inside, frame_of(got, f) + sums[f], 0.0))

    if square:
        shift_column(0)
    if line:
        late.arrived(far, tile)
        late.across(far)
    if square:
        shift_column(1)
    else:
        for number, peer in enumerate(tile_peers):
            column_arrived(early, peer)
            column_arrived(edge, peer)
            make_shift(shift_own, number + 1, peer, 0)

    def stacked(ref, lead, low, count, lanes):
        blocks = [
            ref[lead(index) + (slice(fr * low, fr * (low + count)), lanes)]
            for index in range(clips)
        ]
        return jnp.concatenate(blocks, axis=0)

    contract = (((0,), (0,)), ((), ()))
    whole = slice(0, channels)

    def products(shift, slot, source_tile, dest_tile, tap, side):
        count = frames - 2 + tap
        _, _, first = shares(dest_tile)
        shift_at = lambda index: (slot, index)
        late_at = lambda index: (index, source_tile)
        lanes = whole if side is None else slice(half * side, half * (side + 1))
        width = lanes.stop - lanes.start
        if_encoder = lambda: lax.dot_general(
            stacked(shift, shift_at, 0, count, whole),
            stacked(late_all, late_at, frames - count, count, lanes),
            contract,
            preferred_element_type=F32,
        )

        def if_decoder():
            acts = stacked(late_all, late_at, 0, count, whole)
            sums = [
                lax.dot_general(
                    acts,
                    stacked(
                        shift,
                        shift_at,
                        frames - count,
                        count,
                        slice(base + lanes.start, base + lanes.stop),
                    ),
                    contract,
                    preferred_element_type=F32,
                )
                for base in (0, channels)
            ]
            rows = lax.broadcasted_iota(jnp.int32, (channels, width), 0)
            return jnp.where(rows >= first, sums[0], sums[1])

        return if_encoder, if_decoder

    def keep(tap, low, left, values):
        high, right = low + values.shape[0], left + values.shape[1]
        result[tap, low:high, left:right] = values
        result[tap, channels + low : channels + high, left:right] = values

    def window(tap, dest_tile, width):
        _, _, first = shares(dest_tile)
        if row_total % 16 == 0:
            first = pl.multiple_of(first, 16)
            return result[tap, pl.ds(first, row_total), :width]
        turned = pltpu.roll(result[tap, :channels, :width], (channels - first) % channels, 0)
        return turned[:row_total]

    def half_encoder(sources, tap, side):
        count = frames - 2 + tap
        lanes = slice(half * side, half * (side + 1))
        moved = [
            stacked(ref, lambda index: (slot, index), 0, count, whole) for ref, slot, _ in sources
        ]
        ups = [
            stacked(late_all, lambda index: (index, source), frames - count, count, lanes)
            for _, _, source in sources
        ]
        return lax.dot_general(
            jnp.concatenate(moved, axis=0),
            jnp.concatenate(ups, axis=0),
            contract,
            preferred_element_type=F32,
        )

    def half_decoder(sources, tap, side, first):
        count = frames - 2 + tap
        lanes = slice(half * side, half * (side + 1))
        acts = jnp.concatenate(
            [
                stacked(late_all, lambda index: (index, source), 0, count, lanes)
                for _, _, source in sources
            ],
            axis=0,
        )
        sums = []
        for base in (0, channels):
            moved = [
                stacked(
                    ref,
                    lambda index: (slot, index),
                    frames - count,
                    count,
                    slice(base, base + channels),
                )
                for ref, slot, _ in sources
            ]
            sums.append(
                lax.dot_general(
                    acts,
                    jnp.concatenate(moved, axis=0),
                    contract,
                    preferred_element_type=F32,
                )
            )
        ids = lax.broadcasted_iota(jnp.int32, (half, channels), 0) + half * side
        return jnp.where(ids >= first, sums[0], sums[1])

    def portion(ref, other, side, place):
        return pltpu.make_async_remote_copy(
            src_ref=ref.at[side],
            dst_ref=other.at[side],
            send_sem=part_out.at[side],
            recv_sem=part_in.at[side],
            device_id=place,
            device_id_type=MESH,
        )

    if square:
        for side in range(2):
            peer, dest = tile_peers[side], tile_peers[1 - side]
            column_arrived(late, peer, side)
            sources = [(shift_far, 2 * side, tile), (shift_far, 2 * side + 1, peer)]

            @pl.when(is_encoder)
            def _():
                for tap in range(3):
                    keep(tap, 0, 0, half_encoder(sources, tap, side))
                    part_send[side, tap] = window(tap, dest, half).astype(BF16)

            @pl.when(is_decoder)
            def _():
                first = shares(dest)[2]
                for tap in range(3):
                    values = half_decoder(sources, tap, side, first)
                    rows_send[side, tap] = values.astype(BF16)

            place = (section, clip, dest)
            go(portion(part_send, part_recv, side, place), is_encoder)
            go(portion(rows_send, rows_recv, side, place), is_decoder)

        own_first = shares(tile)[2]
        own_sources = [
            [(shift_own, 0, tile), (shift_own, side + 1, tile_peers[side])] for side in range(2)
        ]

        @pl.when(is_encoder)
        def _():
            for side in range(2):
                for tap in range(3):
                    keep(tap, 0, half * side, half_encoder(own_sources[side], tap, side))
            for side in range(2):
                portion(part_recv, part_recv, side, twin).wait_recv()

        @pl.when(is_decoder)
        def _():
            for side in range(2):
                for tap in range(3):
                    values = half_decoder(own_sources[side], tap, side, own_first)
                    result[tap, half * side : half * (side + 1)] = values
            for side in range(2):
                portion(rows_recv, rows_recv, side, twin).wait_recv()
                for tap in range(3):
                    values = result[tap, half * side : half * (side + 1)]
                    keep(tap, half * side, 0, values + rows_recv[side, tap].astype(F32))

    else:
        for peer in tile_peers:
            column_arrived(late, peer)
        for tap in range(3):
            result[tap, :channels] = jnp.zeros((channels, channels), F32)
            for which, chosen in ((0, is_encoder), (1, is_decoder)):

                @pl.when(chosen)
                def _():
                    @pl.loop(0, tiles)
                    def _(slot):
                        source = (tile + slot) % tiles
                        result[tap, :channels] += products(
                            shift_own, slot, source, tile, tap, None
                        )[which]()

            result[tap, channels : 2 * channels] = result[tap, :channels]

    def write_grads(tap, values):
        for side in range(2):
            low = 2 * row_total * tap + side
            grads_ref[pl.ds(low, row_total, stride=2), :] = values[
                :, half * side : half * (side + 1)
            ]

    if square:

        @pl.when(is_encoder)
        def _():
            for tap in range(3):
                parts = [part_recv[side, tap].astype(F32) for side in range(2)]
                write_grads(tap, window(tap, tile, channels) + jnp.concatenate(parts, axis=1))

        @pl.when(is_decoder)
        def _():
            for tap in range(3):
                write_grads(tap, window(tap, tile, channels))

    else:
        for tap in range(3):
            write_grads(tap, window(tap, tile, channels))

    for copy, only in started:
        if only is None:
            copy.wait_send()
        else:
            pl.when(only)(copy.wait_send)


def place_kernel(out_from, grads_from, out_to, grads_to, sems):
    copies = [
        pltpu.make_async_copy(grads_from, grads_to, sems.at[0]),
        pltpu.make_async_copy(out_from, out_to, sems.at[1]),
    ]
    for copy in copies:
        copy.start()
    for copy in copies:
        copy.wait()


def local(video, cotangent, weights, neighbours, rows_used, cols_used):
    frames, height, columns, channels = video.shape[2:]
    clips, tiles = lax.axis_size("clip"), lax.axis_size("tile")
    row_total = 9 * channels // (clips * tiles)
    rows = frames * height * columns
    dims = (clips, tiles, frames, height, columns, channels, row_total)
    edge_rows = 2 * columns * (frames + 1)
    padded = 2 * LEAD + frames * (height + 2) * columns
    peers = 2 if tiles == 4 else tiles - 1
    count = (clips - 1 + (1 if clips == 4 else 0)) + peers + (clips - 1) * peers
    dma = pltpu.SemaphoreType.DMA
    own_out, summed = pl.pallas_call(
        functools.partial(block_kernel, dims),
        out_shape=(
            jax.ShapeDtypeStruct((frames, height, columns, channels), BF16),
            jax.ShapeDtypeStruct((3 * row_total * 2, channels // 2), F32),
        ),
        in_specs=[pl.BlockSpec(memory_space=pltpu.VMEM)] * 2 + [pl.BlockSpec(memory_space=pltpu.HBM)] * 4,
        out_specs=(pl.BlockSpec(memory_space=pltpu.VMEM),) * 2,
        scratch_shapes=[
            pltpu.SMEM((1, 1, 2), jnp.int32),
            pltpu.VMEM((frames, height, columns, channels), BF16),
            pltpu.VMEM((frames, height, columns, channels), BF16),
            pltpu.VMEM((27, channels, channels), BF16),
            pltpu.VMEM((rows, channels), F32),
            pltpu.VMEM((padded, channels), F32),
            pltpu.VMEM((3, 2 * rows, 128), BF16),
            pltpu.VMEM((3, 2 * rows, 128), F32),
            pltpu.VMEM((3, 2 * rows, 128), F32),
            pltpu.VMEM((3, rows, 3 * channels), BF16),
            pltpu.VMEM((clips, tiles, rows, channels), BF16),
            pltpu.VMEM((clips, tiles, edge_rows, channels), BF16),
            pltpu.VMEM((clips, tiles, rows, channels), BF16),
            pltpu.VMEM((tiles, edge_rows, channels), BF16),
            pltpu.VMEM((tiles, edge_rows, channels), BF16),
            pltpu.VMEM((rows, channels), F32),
            pltpu.VMEM((rows, channels), F32),
            pltpu.VMEM((peers + 1, clips, rows, 2 * channels), BF16),
            pltpu.VMEM((4 if tiles == 4 else 1, clips, rows, 2 * channels), BF16),
            pltpu.VMEM((3, 2 * channels, channels), F32),
            pltpu.VMEM((2, 3, row_total, channels // 2), BF16),
            pltpu.VMEM((2, 3, row_total, channels // 2), BF16),
            pltpu.VMEM((2, 3, channels // 2, channels), BF16),
            pltpu.VMEM((2, 3, channels // 2, channels), BF16),
            dma((4,)),
            dma((count,)),
            dma((count,)),
            dma((count,)),
            dma((clips, tiles)),
            dma((clips, tiles)),
            dma((clips, tiles)),
            dma((2, tiles - 1)),
            dma((2, tiles)),
            dma((2,)),
            dma((2,)),
            dma((2,)),
        ],
        compiler_params=pltpu.CompilerParams(
            collective_id=0,
            has_side_effects=True,
            vmem_limit_bytes=(53 if tiles == 4 else 56) * 2**20,
        ),
    )(rows_used, cols_used[None], neighbours, video, cotangent, weights)
    own_out, summed = pl.pallas_call(
        place_kernel,
        out_shape=(
            jax.ShapeDtypeStruct(own_out.shape, BF16),
            jax.ShapeDtypeStruct(summed.shape, F32),
        ),
        in_specs=[pl.BlockSpec(memory_space=pl.ANY)] * 2,
        out_specs=(pl.BlockSpec(memory_space=pltpu.HBM),) * 2,
        scratch_shapes=[dma((2,))],
        compiler_params=pltpu.CompilerParams(vmem_limit_bytes=2**20),
    )(own_out, summed)
    return (own_out[None, None, None], summed.reshape(1, 3, row_total * channels))


def solution(mesh):
    in_specs = (
        P("clip", "tile", None, None, None, None),
        P("clip", "tile", None, None, None, None),
        P("segment", None, None, None),
        P("clip", "tile", None),
        P("clip", "tile"),
        P("clip"),
    )
    out_specs = (
        P("segment", "clip", "tile", None, None, None, None),
        P("segment", None, ("clip", "tile")),
    )
    return jax.shard_map(local, mesh=mesh, in_specs=in_specs, out_specs=out_specs, check_vma=False)
```

```python
import functools

import jax
import jax.numpy as jnp
from jax import lax
from jax.experimental import pallas as pl
from jax.experimental.pallas import tpu as pltpu
from jax.sharding import PartitionSpec as P

MESH = pl.DeviceIdType.MESH
F32, BF16 = jnp.float32, jnp.bfloat16
LEAD = 8


def silu(values):
    return values / (1.0 + jnp.exp(-values))


def silu_grad(values):
    sigmoid = 1.0 / (1.0 + jnp.exp(-values))
    return sigmoid * (1.0 + values * (1.0 - sigmoid))


def share_of(clip, tile, tiles, row_total, channels):
    start = (clip * tiles + tile) * row_total
    return start // channels, start % channels


def block_kernel(
    dims,
    rows_ref,
    cols_ref,
    near_hbm,
    video_hbm,
    cot_hbm,
    weight_hbm,
    out_ref,
    grads_ref,
    near_ref,
    video,
    cot,
    weight,
    flat,
    wide,
    main_sel,
    rest_sel,
    under_sel,
    taps_mat,
    early_all,
    edge_all,
    late_all,
    halo_one,
    halo_two,
    give,
    got,
    shift_own,
    shift_far,
    result,
    part_send,
    part_recv,
    rows_send,
    rows_recv,
    load_sem,
    early_out,
    edge_out,
    late_out,
    early_in,
    edge_in,
    late_in,
    halo_out,
    halo_in,
    swap_sem,
    part_out,
    part_in,
):
    clips, tiles, frames, height, columns, channels, row_total = dims
    fr = height * columns
    tall = fr + 2 * columns
    rows = frames * fr
    half = channels // 2
    edge_half = columns * (frames + 1)
    section = lax.axis_index("segment")
    clip = lax.axis_index("clip")
    tile = lax.axis_index("tile")
    line = clips == 4
    square = tiles == 4
    inner = (clip + 1) // 2 % 2 == 1

    if line:
        near, over, far = clip + 1 - 2 * (clip % 2), (clip + 2) % 4, 3 - clip
        clip_peers = [over, far, near]
    else:
        clip_peers = [(clip + step) % clips for step in range(1, clips)]
    if square:
        beside, below = tile + 1 - 2 * (tile % 2), (tile + 2) % 4
        tile_peers = [beside, below]
        halo_peers = [beside, below, 3 - tile]
    else:
        tile_peers = halo_peers = [(tile + step) % tiles for step in range(1, tiles)]

    loads = [
        pltpu.make_async_copy(cot_hbm.at[0, 0], cot, load_sem.at[0]),
        pltpu.make_async_copy(video_hbm.at[0, 0], video, load_sem.at[1]),
        pltpu.make_async_copy(weight_hbm.at[0], weight, load_sem.at[2]),
        pltpu.make_async_copy(near_hbm, near_ref, load_sem.at[3]),
    ]
    for index in (0, 1, 3, 2):
        loads[index].start()

    twin = (1 - section, clip, tile)
    barrier = pltpu.get_barrier_semaphore()
    greeted = [twin]
    greeted += [(section, peer, tile) for peer in clip_peers]
    greeted += [(section, clip, peer) for peer in halo_peers]
    for place in greeted:
        pl.semaphore_signal(barrier, inc=1, device_id=place, device_id_type=MESH)

    row_count = jnp.full((fr, channels), rows_ref[0, 0], jnp.int32)
    col_count = cols_ref[0]
    ids = lax.broadcasted_iota(jnp.int32, (fr, channels), 0)
    column = ids % columns
    row_id = ids // columns
    inside = (row_id < row_count) & (column < col_count)

    started = []

    def transfer(ref, slot, send_sem, recv_sem, place):
        return pltpu.make_async_remote_copy(
            src_ref=ref.at[slot],
            dst_ref=ref.at[slot],
            send_sem=send_sem,
            recv_sem=recv_sem,
            device_id=place,
            device_id_type=MESH,
        )

    def go(copy, only=None):
        started.append((copy, only))
        if only is None:
            copy.start()
        else:
            pl.when(only)(copy.start)

    class Field:
        def __init__(self, ref, outs, ins, halved=False):
            self.ref, self.outs, self.ins, self.used = ref, outs, ins, 0
            self.halved = halved

        def part(self, slot_clip, slot_tile, side):
            if side is None:
                return slot_clip, slot_tile
            return slot_clip, slot_tile, slice(None), pl.ds(half * side, half)

        def send(self, slot_clip, place, only=None, side=None):
            copy = transfer(
                self.ref,
                self.part(slot_clip, tile, side),
                self.outs.at[self.used],
                self.ins.at[slot_clip, tile],
                place,
            )
            self.used += 1
            go(copy, only)

        def send_own(self):
            for peer in clip_peers:
                skip = line and peer is far
                self.send(clip, (section, peer, tile), inner if skip else None)
            self.across(clip)

        def arrived(self, slot_clip, slot_tile, side=None):
            transfer(
                self.ref,
                self.part(slot_clip, slot_tile, side),
                self.outs.at[0],
                self.ins.at[slot_clip, slot_tile],
                twin,
            ).wait_recv()

        def along(self):
            self.send(over, (section, near, tile), inner)

        def across(self, slot_clip):
            for number, peer in enumerate(tile_peers):
                side = number if self.halved else None
                self.send(slot_clip, (section, clip, peer), None, side)

    early = Field(early_all, early_out, early_in)
    edge = Field(edge_all, edge_out, edge_in)
    late = Field(late_all, late_out, late_in, square)

    def read_field(source, target):
        for frame in range(frames):
            for row in range(height):
                low = fr * frame + columns * row
                target[low : low + columns] = source[frame, row].astype(F32)

    def frame_of(ref, frame):
        return ref[fr * frame : fr * (frame + 1)]

    def ends_of(ref):
        leading = [ref[fr * f : fr * f + columns] for f in range(frames)]
        trailing = []
        for f in range(frames):
            last = leading[f]
            for row in range(1, height):
                low = fr * f + columns * row
                last = jnp.where(row_count[:columns] == row + 1, ref[low : low + columns], last)
            trailing.append(last)
        blank = jnp.zeros((columns, channels), F32)
        return jnp.concatenate(leading + [blank] + trailing + [blank], axis=0)

    def send_halo(ref, number, only=None):
        for index, peer in enumerate(halo_peers):
            copy = transfer(
                ref,
                tile,
                halo_out.at[number, index],
                halo_in.at[number, tile],
                (section, clip, peer),
            )
            go(copy, only)

    def take_halo(ref, number):
        for peer in halo_peers:
            transfer(ref, peer, halo_out.at[number, 0], halo_in.at[number, peer], twin).wait_recv()
        upper_tile = near_ref[0, 0, 0]
        lower_tile = near_ref[0, 0, 1]
        above = ref[jnp.minimum(upper_tile, tiles - 1)].astype(F32)
        under = ref[jnp.minimum(lower_tile, tiles - 1)].astype(F32)
        above = jnp.where(upper_tile < tiles, above[edge_half : 2 * edge_half], 0.0)
        under = jnp.where(lower_tile < tiles, under[:edge_half], 0.0)
        return above, under

    def repeated(block, count):
        return jnp.concatenate([block] * count, axis=0)

    def write_frame(target, frame, main, top, bottom, hit, full):
        base = LEAD + tall * frame
        target[base : base + columns] = top
        target[base + columns : base + columns + fr] = jnp.where(
            hit, repeated(bottom, height), main
        )
        target[base + columns + fr : base + tall] = jnp.where(full, bottom, 0.0)

    def pad_own(above, under):
        hit = row_id == row_count
        full = row_count[:columns] == height
        for f in range(frames):
            low = columns * f
            write_frame(
                wide,
                f,
                frame_of(flat, f),
                above[low : low + columns],
                under[low : low + columns],
                hit,
                full,
            )

    def make_taps():
        for f in range(frames):
            for row_off in range(3):
                for col_off in range(3):
                    start = LEAD + tall * f + columns * row_off + col_off - 1
                    block = wide[start : start + fr]
                    if col_off == 0:
                        block = jnp.where(column > 0, block, 0.0)
                    if col_off == 2:
                        block = jnp.where(column < columns - 1, block, 0.0)
                    taps_mat[
                        row_off,
                        fr * f : fr * (f + 1),
                        channels * col_off : channels * (col_off + 1),
                    ] = block.astype(BF16)

    def conv_front():
        sums = [jnp.zeros((fr, channels), F32) for _ in range(frames)]
        for depth_off in range(3):
            count = frames - 2 + depth_off
            part = jnp.zeros((fr * count, channels), F32)
            for row_off in range(3):
                tap = 9 * depth_off + 3 * row_off
                part += jnp.dot(
                    taps_mat[row_off, : fr * count, :],
                    weight[tap : tap + 3].reshape(3 * channels, channels),
                    preferred_element_type=F32,
                )
            for n in range(count):
                sums[frames - count + n] += part[fr * n : fr * (n + 1)]
        return sums

    def conv_back():
        sums = [jnp.zeros((fr, channels), F32) for _ in range(frames)]
        for depth_off in range(3):
            count = frames - depth_off
            part = jnp.zeros((fr * count, channels), F32)
            for row_off in range(3):
                for col_off in range(3):
                    tap = 9 * depth_off + 3 * row_off + col_off
                    part += lax.dot_general(
                        taps_mat[
                            row_off,
                            fr * depth_off :,
                            channels * col_off : channels * (col_off + 1),
                        ],
                        weight[26 - tap],
                        (((1,), (1,)), ((), ())),
                        preferred_element_type=F32,
                    )
            for n in range(count):
                sums[n] += part[fr * n : fr * (n + 1)]
        return sums

    def write_out(frame, values):
        for row in range(height):
            out_ref[frame, row] = values[columns * row : columns * (row + 1)].astype(BF16)

    def shares(dest_tile):
        tap, first = share_of(clip, dest_tile, tiles, row_total, channels)
        return tap, jnp.minimum(tap + 1, 8), first

    dests = [tile] + (tile_peers if square else [])

    def make_selections():
        place = lax.broadcasted_iota(jnp.int32, (rows, 128), 0)
        lane = lax.broadcasted_iota(jnp.int32, (rows, 128), 1)
        col_id = place % columns
        line_id = place // columns
        frame_id = line_id // height
        line_id = line_id - height * frame_id
        for dest, dest_tile in enumerate(dests):
            for half_id, tap in enumerate(shares(dest_tile)[:2]):
                row_off, col_off = tap // 3, tap % 3
                row_off = row_off + section * (2 - 2 * row_off) - 1
                col_off = col_off + section * (2 - 2 * col_off) - 1
                there, beyond = line_id + row_off, col_id + col_off
                valid = (beyond >= 0) & (beyond < columns)
                main = jnp.where(
                    valid & (there >= 0) & (there < height),
                    place + columns * row_off + col_off,
                    -1,
                )
                rim = jnp.where(valid, columns * frame_id + beyond, -4 * rows)
                top = jnp.where(there == -1, rim + rows, -1)
                low = rows * half_id
                main_sel[dest, low : low + rows] = jnp.where(lane == main, 1.0, 0.0).astype(BF16)
                rest = (lane + 128 == main) | (lane + 128 == top)
                rest_sel[dest, low : low + rows] = jnp.where(rest, 1.0, 0.0)
                under_sel[dest, low : low + rows] = jnp.where(
                    lane + 128 == rim + rows + edge_half, there.astype(F32), -5.0
                )

    is_encoder = section == 0
    is_decoder = section != 0
    wide[...] = jnp.zeros(wide.shape, F32)
    loads[0].wait()
    loads[1].wait()

    @pl.when(is_encoder)
    def _():
        read_field(video, flat)
        for f in range(frames):
            values = jnp.where(inside, frame_of(flat, f), 0.0)
            active = silu(values).astype(BF16)
            early_all[clip, tile, fr * f : fr * (f + 1)] = active
            flat[fr * f : fr * (f + 1)] = active.astype(F32)

    @pl.when(is_decoder)
    def _():
        read_field(cot, flat)
        for f in range(frames):
            values = jnp.where(inside, frame_of(flat, f), 0.0)
            early_all[clip, tile, fr * f : fr * (f + 1)] = values.astype(BF16)
            flat[fr * f : fr * (f + 1)] = values

    halo_one[tile] = ends_of(flat).astype(BF16)
    pl.semaphore_wait(barrier, len(greeted))
    send_halo(halo_one, 0)
    early.send_own()
    make_selections()

    loads[3].wait()
    above, under = take_halo(halo_one, 0)
    pad_own(above, under)
    count_rows = row_count[:columns].astype(F32)
    edge_all[clip, tile] = jnp.concatenate(
        [above[: edge_half - columns], count_rows, under], axis=0
    ).astype(BF16)
    edge.send_own()
    make_taps()
    loads[2].wait()

    @pl.when(is_encoder)
    def _():
        read_field(video, flat)
        sums = conv_front()
        for f in range(frames):
            values = jnp.where(inside, frame_of(flat, f) + sums[f], 0.0).astype(BF16)
            give[fr * f : fr * (f + 1)] = values.astype(F32)

    @pl.when(is_decoder)
    def _():
        sums = conv_back()
        for f in range(frames):
            give[fr * f : fr * (f + 1)] = sums[f]

    swap = pltpu.make_async_remote_copy(
        src_ref=give,
        dst_ref=got,
        send_sem=swap_sem.at[0],
        recv_sem=swap_sem.at[1],
        device_id=twin,
        device_id_type=MESH,
    )
    go(swap)

    @pl.when(is_encoder)
    def _():
        read_field(cot, flat)
        for f in range(frames):
            write_out(f, frame_of(give, f))

    if line:
        early.arrived(over, tile)
        early.along()
        early.across(over)
        early.arrived(near, tile)
        early.across(near)
    swap.wait_recv()

    @pl.when(is_encoder)
    def _():
        for f in range(frames):
            target = frame_of(flat, f)
            values = target + silu_grad(frame_of(give, f)) * frame_of(got, f)
            late_all[clip, tile, fr * f : fr * (f + 1)] = jnp.where(inside, values, 0.0).astype(
                BF16
            )

    @pl.when(is_decoder)
    def _():
        for f in range(frames):
            active = silu(frame_of(got, f)).astype(BF16)
            late_all[clip, tile, fr * f : fr * (f + 1)] = active
            flat[fr * f : fr * (f + 1)] = active.astype(F32)
        halo_two[tile] = ends_of(flat).astype(BF16)

    def make_shift(target, slot, source_tile, dest):
        first = shares(dests[dest])[2]
        lane = lax.broadcasted_iota(jnp.int32, (rows, channels), 1)
        keep_first = (lane >= first) | is_decoder

        @pl.loop(0, clips, unroll=clips if square else 1)
        def _(index):
            rim = edge_all[index, source_tile]
            count = rim.astype(F32)[edge_half - columns : edge_half - columns + 1, :128]
            rest = rest_sel[dest] + jnp.where(under_sel[dest] == count, 1.0, 0.0)
            picks = jnp.concatenate([main_sel[dest], rest.astype(BF16)], axis=1)
            field = jnp.concatenate([early_all[index, source_tile], rim], axis=0)
            moved = jnp.dot(
                picks[:, : rows + 2 * edge_half], field, preferred_element_type=F32
            )
            picked = jnp.where(keep_first, moved[:rows], moved[rows:])
            target[slot, index, :, :channels] = picked.astype(BF16)
            target[slot, index, :, channels:] = moved[rows:].astype(BF16)

    def column_arrived(field, source_tile, side=None):
        for index in range(clips):
            field.arrived(index, source_tile, side)

    def shift_column(number):
        peer = tile_peers[number]
        column_arrived(early, peer)
        column_arrived(edge, peer)
        make_shift(shift_far, 2 * number + 1, peer, 2 - number)
        make_shift(shift_own, number + 1, peer, 0)

    late.send_own()
    send_halo(halo_two, 1, is_decoder)
    if line:
        edge.arrived(over, tile)
        edge.along()

    for peer in [far] if line else clip_peers:
        early.arrived(peer, tile)
        early.across(peer)
    for peer in reversed(clip_peers):
        if not (line and peer is over):
            edge.arrived(peer, tile)
        edge.across(peer)

    make_shift(shift_own, 0, tile, 0)
    if square:
        for number in range(2):
            make_shift(shift_far, 2 * number, tile, 2 - number)
    for peer in [over, near] if line else clip_peers:
        late.arrived(peer, tile)
        if line and peer is over:
            late.along()
        late.across(peer)

    @pl.when(is_decoder)
    def _():
        pad_own(*take_halo(halo_two, 1))
        make_taps()
        sums = conv_front()
        for f in range(frames):
            write_out(f, jnp.where(inside, frame_of(got, f) + sums[f], 0.0))

    if square:
        shift_column(0)
    if line:
        late.arrived(far, tile)
        late.across(far)
    if square:
        shift_column(1)
    else:
        for number, peer in enumerate(tile_peers):
            column_arrived(early, peer)
            column_arrived(edge, peer)
            make_shift(shift_own, number + 1, peer, 0)

    def stacked(ref, lead, low, count, lanes):
        blocks = [
            ref[lead(index) + (slice(fr * low, fr * (low + count)), lanes)]
            for index in range(clips)
        ]
        return jnp.concatenate(blocks, axis=0)

    contract = (((0,), (0,)), ((), ()))
    whole = slice(0, channels)

    def products(shift, slot, source_tile, dest_tile, tap, side):
        count = frames - 2 + tap
        _, _, first = shares(dest_tile)
        shift_at = lambda index: (slot, index)
        late_at = lambda index: (index, source_tile)
        lanes = whole if side is None else slice(half * side, half * (side + 1))
        width = lanes.stop - lanes.start
        if_encoder = lambda: lax.dot_general(
            stacked(shift, shift_at, 0, count, whole),
            stacked(late_all, late_at, frames - count, count, lanes),
            contract,
            preferred_element_type=F32,
        )

        def if_decoder():
            acts = stacked(late_all, late_at, 0, count, whole)
            sums = [
                lax.dot_general(
                    acts,
                    stacked(
                        shift,
                        shift_at,
                        frames - count,
                        count,
                        slice(base + lanes.start, base + lanes.stop),
                    ),
                    contract,
                    preferred_element_type=F32,
                )
                for base in (0, channels)
            ]
            rows = lax.broadcasted_iota(jnp.int32, (channels, width), 0)
            return jnp.where(rows >= first, sums[0], sums[1])

        return if_encoder, if_decoder

    def keep(tap, low, left, values):
        high, right = low + values.shape[0], left + values.shape[1]
        result[tap, low:high, left:right] = values
        result[tap, channels + low : channels + high, left:right] = values

    def window(tap, dest_tile, width):
        _, _, first = shares(dest_tile)
        if row_total % 16 == 0:
            first = pl.multiple_of(first, 16)
            return result[tap, pl.ds(first, row_total), :width]
        turned = pltpu.roll(result[tap, :channels, :width], (channels - first) % channels, 0)
        return turned[:row_total]

    def half_encoder(sources, tap, side):
        count = frames - 2 + tap
        lanes = slice(half * side, half * (side + 1))
        moved = [
            stacked(ref, lambda index: (slot, index), 0, count, whole) for ref, slot, _ in sources
        ]
        ups = [
            stacked(late_all, lambda index: (index, source), frames - count, count, lanes)
            for _, _, source in sources
        ]
        return lax.dot_general(
            jnp.concatenate(moved, axis=0),
            jnp.concatenate(ups, axis=0),
            contract,
            preferred_element_type=F32,
        )

    def half_decoder(sources, tap, side, first):
        count = frames - 2 + tap
        lanes = slice(half * side, half * (side + 1))
        acts = jnp.concatenate(
            [
                stacked(late_all, lambda index: (index, source), 0, count, lanes)
                for _, _, source in sources
            ],
            axis=0,
        )
        sums = []
        for base in (0, channels):
            moved = [
                stacked(
                    ref,
                    lambda index: (slot, index),
                    frames - count,
                    count,
                    slice(base, base + channels),
                )
                for ref, slot, _ in sources
            ]
            sums.append(
                lax.dot_general(
                    acts,
                    jnp.concatenate(moved, axis=0),
                    contract,
                    preferred_element_type=F32,
                )
            )
        ids = lax.broadcasted_iota(jnp.int32, (half, channels), 0) + half * side
        return jnp.where(ids >= first, sums[0], sums[1])

    def portion(ref, other, side, place):
        return pltpu.make_async_remote_copy(
            src_ref=ref.at[side],
            dst_ref=other.at[side],
            send_sem=part_out.at[side],
            recv_sem=part_in.at[side],
            device_id=place,
            device_id_type=MESH,
        )

    if square:
        for side in range(2):
            peer, dest = tile_peers[side], tile_peers[1 - side]
            column_arrived(late, peer, side)
            sources = [(shift_far, 2 * side, tile), (shift_far, 2 * side + 1, peer)]

            @pl.when(is_encoder)
            def _():
                for tap in range(3):
                    keep(tap, 0, 0, half_encoder(sources, tap, side))
                    part_send[side, tap] = window(tap, dest, half).astype(BF16)

            @pl.when(is_decoder)
            def _():
                first = shares(dest)[2]
                for tap in range(3):
                    values = half_decoder(sources, tap, side, first)
                    rows_send[side, tap] = values.astype(BF16)

            place = (section, clip, dest)
            go(portion(part_send, part_recv, side, place), is_encoder)
            go(portion(rows_send, rows_recv, side, place), is_decoder)

        own_first = shares(tile)[2]
        own_sources = [
            [(shift_own, 0, tile), (shift_own, side + 1, tile_peers[side])] for side in range(2)
        ]

        @pl.when(is_encoder)
        def _():
            for side in range(2):
                for tap in range(3):
                    keep(tap, 0, half * side, half_encoder(own_sources[side], tap, side))
            for side in range(2):
                portion(part_recv, part_recv, side, twin).wait_recv()

        @pl.when(is_decoder)
        def _():
            for side in range(2):
                for tap in range(3):
                    values = half_decoder(own_sources[side], tap, side, own_first)
                    result[tap, half * side : half * (side + 1)] = values
            for side in range(2):
                portion(rows_recv, rows_recv, side, twin).wait_recv()
                for tap in range(3):
                    values = result[tap, half * side : half * (side + 1)]
                    keep(tap, half * side, 0, values + rows_recv[side, tap].astype(F32))

    else:
        for peer in tile_peers:
            column_arrived(late, peer)
        for tap in range(3):
            result[tap, :channels] = jnp.zeros((channels, channels), F32)
            for which, chosen in ((0, is_encoder), (1, is_decoder)):

                @pl.when(chosen)
                def _():
                    @pl.loop(0, tiles)
                    def _(slot):
                        source = (tile + slot) % tiles
                        result[tap, :channels] += products(
                            shift_own, slot, source, tile, tap, None
                        )[which]()

            result[tap, channels : 2 * channels] = result[tap, :channels]

    def write_grads(tap, values):
        for side in range(2):
            low = 2 * row_total * tap + side
            grads_ref[pl.ds(low, row_total, stride=2), :] = values[
                :, half * side : half * (side + 1)
            ]

    if square:

        @pl.when(is_encoder)
        def _():
            for tap in range(3):
                parts = [part_recv[side, tap].astype(F32) for side in range(2)]
                write_grads(tap, window(tap, tile, channels) + jnp.concatenate(parts, axis=1))

        @pl.when(is_decoder)
        def _():
            for tap in range(3):
                write_grads(tap, window(tap, tile, channels))

    else:
        for tap in range(3):
            write_grads(tap, window(tap, tile, channels))

    for copy, only in started:
        if only is None:
            copy.wait_send()
        else:
            pl.when(only)(copy.wait_send)


def place_kernel(out_from, grads_from, out_to, grads_to, sems):
    copies = [
        pltpu.make_async_copy(grads_from, grads_to, sems.at[0]),
        pltpu.make_async_copy(out_from, out_to, sems.at[1]),
    ]
    for copy in copies:
        copy.start()
    for copy in copies:
        copy.wait()


def local(video, cotangent, weights, neighbours, rows_used, cols_used):
    frames, height, columns, channels = video.shape[2:]
    clips, tiles = lax.axis_size("clip"), lax.axis_size("tile")
    row_total = 9 * channels // (clips * tiles)
    rows = frames * height * columns
    dims = (clips, tiles, frames, height, columns, channels, row_total)
    edge_rows = 2 * columns * (frames + 1)
    padded = 2 * LEAD + frames * (height + 2) * columns
    peers = 2 if tiles == 4 else tiles - 1
    count = (clips - 1 + (1 if clips == 4 else 0)) + peers + (clips - 1) * peers
    dma = pltpu.SemaphoreType.DMA
    held = [
        pltpu.with_memory_space_constraint(array, pltpu.HBM)
        for array in (neighbours, video, cotangent, weights)
    ]
    own_out, summed = pl.pallas_call(
        functools.partial(block_kernel, dims),
        out_shape=(
            jax.ShapeDtypeStruct((frames, height, columns, channels), BF16),
            jax.ShapeDtypeStruct((3 * row_total * 2, channels // 2), F32),
        ),
        in_specs=[pl.BlockSpec(memory_space=pltpu.SMEM)] * 2 + [pl.BlockSpec(memory_space=pltpu.HBM)] * 4,
        out_specs=(pl.BlockSpec(memory_space=pltpu.VMEM),) * 2,
        scratch_shapes=[
            pltpu.SMEM((1, 1, 2), jnp.int32),
            pltpu.VMEM((frames, height, columns, channels), BF16),
            pltpu.VMEM((frames, height, columns, channels), BF16),
            pltpu.VMEM((27, channels, channels), BF16),
            pltpu.VMEM((rows, channels), F32),
            pltpu.VMEM((padded, channels), F32),
            pltpu.VMEM((3, 2 * rows, 128), BF16),
            pltpu.VMEM((3, 2 * rows, 128), F32),
            pltpu.VMEM((3, 2 * rows, 128), F32),
            pltpu.VMEM((3, rows, 3 * channels), BF16),
            pltpu.VMEM((clips, tiles, rows, channels), BF16),
            pltpu.VMEM((clips, tiles, edge_rows, channels), BF16),
            pltpu.VMEM((clips, tiles, rows, channels), BF16),
            pltpu.VMEM((tiles, edge_rows, channels), BF16),
            pltpu.VMEM((tiles, edge_rows, channels), BF16),
            pltpu.VMEM((rows, channels), F32),
            pltpu.VMEM((rows, channels), F32),
            pltpu.VMEM((peers + 1, clips, rows, 2 * channels), BF16),
            pltpu.VMEM((4 if tiles == 4 else 1, clips, rows, 2 * channels), BF16),
            pltpu.VMEM((3, 2 * channels, channels), F32),
            pltpu.VMEM((2, 3, row_total, channels // 2), BF16),
            pltpu.VMEM((2, 3, row_total, channels // 2), BF16),
            pltpu.VMEM((2, 3, channels // 2, channels), BF16),
            pltpu.VMEM((2, 3, channels // 2, channels), BF16),
            dma((4,)),
            dma((count,)),
            dma((count,)),
            dma((count,)),
            dma((clips, tiles)),
            dma((clips, tiles)),
            dma((clips, tiles)),
            dma((2, tiles - 1)),
            dma((2, tiles)),
            dma((2,)),
            dma((2,)),
            dma((2,)),
        ],
        compiler_params=pltpu.CompilerParams(
            collective_id=0,
            has_side_effects=True,
            vmem_limit_bytes=(32 if tiles == 4 else 56) * 2**20,
        ),
    )(rows_used, cols_used, *held)
    own_out, summed = pl.pallas_call(
        place_kernel,
        out_shape=(
            jax.ShapeDtypeStruct(own_out.shape, BF16),
            jax.ShapeDtypeStruct(summed.shape, F32),
        ),
        in_specs=[pl.BlockSpec(memory_space=pl.ANY)] * 2,
        out_specs=(pl.BlockSpec(memory_space=pltpu.HBM),) * 2,
        scratch_shapes=[dma((2,))],
        compiler_params=pltpu.CompilerParams(vmem_limit_bytes=2**20),
    )(own_out, summed)
    return (own_out[None, None, None], summed.reshape(1, 3, row_total * channels))


def solution(mesh):
    in_specs = (
        P("clip", "tile", None, None, None, None),
        P("clip", "tile", None, None, None, None),
        P("segment", None, None, None),
        P("clip", "tile", None),
        P("clip", "tile"),
        P("clip"),
    )
    out_specs = (
        P("segment", "clip", "tile", None, None, None, None),
        P("segment", None, ("clip", "tile")),
    )
    return jax.shard_map(local, mesh=mesh, in_specs=in_specs, out_specs=out_specs, check_vma=False)
```

```python
import functools

import jax
import jax.numpy as jnp
from jax import lax
from jax.experimental import pallas as pl
from jax.experimental.pallas import tpu as pltpu
from jax.sharding import PartitionSpec as P

MESH = pl.DeviceIdType.MESH
F32, BF16 = jnp.float32, jnp.bfloat16
LEAD = 8


def silu(values):
    return values / (1.0 + jnp.exp(-values))


def silu_grad(values):
    sigmoid = 1.0 / (1.0 + jnp.exp(-values))
    return sigmoid * (1.0 + values * (1.0 - sigmoid))


def share_of(clip, tile, tiles, row_total, channels):
    start = (clip * tiles + tile) * row_total
    return start // channels, start % channels


def block_kernel(
    dims,
    rows_ref,
    cols_ref,
    near_hbm,
    video_hbm,
    cot_hbm,
    weight_hbm,
    out_ref,
    grads_ref,
    near_ref,
    video,
    cot,
    weight,
    flat,
    wide,
    main_sel,
    rest_sel,
    under_sel,
    taps_mat,
    early_all,
    edge_all,
    late_all,
    halo_one,
    halo_two,
    give,
    got,
    shift_own,
    shift_far,
    result,
    part_send,
    part_recv,
    rows_send,
    rows_recv,
    load_sem,
    early_out,
    edge_out,
    late_out,
    early_in,
    edge_in,
    late_in,
    halo_out,
    halo_in,
    swap_sem,
    part_out,
    part_in,
):
    clips, tiles, frames, height, columns, channels, row_total = dims
    fr = height * columns
    tall = fr + 2 * columns
    rows = frames * fr
    half = channels // 2
    edge_half = columns * (frames + 1)
    section = lax.axis_index("segment")
    clip = lax.axis_index("clip")
    tile = lax.axis_index("tile")
    line = clips == 4
    square = tiles == 4
    inner = (clip + 1) // 2 % 2 == 1

    if line:
        near, over, far = clip + 1 - 2 * (clip % 2), (clip + 2) % 4, 3 - clip
        clip_peers = [over, far, near]
        clip_first, clip_rest = [over], [far, near]
    else:
        clip_peers = [(clip + step) % clips for step in range(1, clips)]
        clip_first, clip_rest = [], clip_peers
    if square:
        beside, below = tile + 1 - 2 * (tile % 2), (tile + 2) % 4
        tile_peers = [beside, below]
        halo_peers = [beside, below, 3 - tile]
    else:
        tile_peers = halo_peers = [(tile + step) % tiles for step in range(1, tiles)]

    loads = [
        pltpu.make_async_copy(cot_hbm.at[0, 0], cot, load_sem.at[0]),
        pltpu.make_async_copy(video_hbm.at[0, 0], video, load_sem.at[1]),
        pltpu.make_async_copy(weight_hbm.at[0], weight, load_sem.at[2]),
        pltpu.make_async_copy(near_hbm, near_ref, load_sem.at[3]),
    ]
    for index in (0, 1, 3, 2):
        loads[index].start()

    twin = (1 - section, clip, tile)
    barrier = pltpu.get_barrier_semaphore()
    greeted = [twin]
    greeted += [(section, peer, tile) for peer in clip_peers]
    greeted += [(section, clip, peer) for peer in halo_peers]
    for place in greeted:
        pl.semaphore_signal(barrier, inc=1, device_id=place, device_id_type=MESH)

    row_count = jnp.full((fr, channels), rows_ref[0, 0], jnp.int32)
    col_count = cols_ref[0]
    ids = lax.broadcasted_iota(jnp.int32, (fr, channels), 0)
    column = ids % columns
    row_id = ids // columns
    inside = (row_id < row_count) & (column < col_count)

    started = []

    def transfer(ref, slot, send_sem, recv_sem, place):
        return pltpu.make_async_remote_copy(
            src_ref=ref.at[slot],
            dst_ref=ref.at[slot],
            send_sem=send_sem,
            recv_sem=recv_sem,
            device_id=place,
            device_id_type=MESH,
        )

    def go(copy, only=None):
        started.append((copy, only))
        if only is None:
            copy.start()
        else:
            pl.when(only)(copy.start)

    class Field:
        def __init__(self, ref, outs, ins, halved=False):
            self.ref, self.outs, self.ins, self.used = ref, outs, ins, 0
            self.halved = halved

        def part(self, slot_clip, slot_tile, side):
            if side is None:
                return slot_clip, slot_tile
            return slot_clip, slot_tile, slice(None), pl.ds(half * side, half)

        def send(self, slot_clip, place, only=None, side=None):
            copy = transfer(
                self.ref,
                self.part(slot_clip, tile, side),
                self.outs.at[self.used],
                self.ins.at[slot_clip, tile],
                place,
            )
            self.used += 1
            go(copy, only)

        def send_own(self, peers):
            for peer in peers:
                skip = line and peer is far
                self.send(clip, (section, peer, tile), inner if skip else None)

        def arrived(self, slot_clip, slot_tile, side=None):
            transfer(
                self.ref,
                self.part(slot_clip, slot_tile, side),
                self.outs.at[0],
                self.ins.at[slot_clip, slot_tile],
                twin,
            ).wait_recv()

        def along(self):
            self.send(over, (section, near, tile), inner)

        def across(self, slot_clip):
            for number, peer in enumerate(tile_peers):
                side = number if self.halved else None
                self.send(slot_clip, (section, clip, peer), None, side)

    early = Field(early_all, early_out, early_in)
    edge = Field(edge_all, edge_out, edge_in)
    late = Field(late_all, late_out, late_in, square)

    def read_field(source, target):
        for frame in range(frames):
            for row in range(height):
                low = fr * frame + columns * row
                target[low : low + columns] = source[frame, row].astype(F32)

    def frame_of(ref, frame):
        return ref[fr * frame : fr * (frame + 1)]

    def ends_of(ref):
        leading = [ref[fr * f : fr * f + columns] for f in range(frames)]
        trailing = []
        for f in range(frames):
            last = leading[f]
            for row in range(1, height):
                low = fr * f + columns * row
                last = jnp.where(row_count[:columns] == row + 1, ref[low : low + columns], last)
            trailing.append(last)
        blank = jnp.zeros((columns, channels), F32)
        return jnp.concatenate(leading + [blank] + trailing + [blank], axis=0)

    def send_halo(ref, number, only=None):
        for index, peer in enumerate(halo_peers):
            copy = transfer(
                ref,
                tile,
                halo_out.at[number, index],
                halo_in.at[number, tile],
                (section, clip, peer),
            )
            go(copy, only)

    def take_halo(ref, number):
        for peer in halo_peers:
            transfer(ref, peer, halo_out.at[number, 0], halo_in.at[number, peer], twin).wait_recv()
        upper_tile = near_ref[0, 0, 0]
        lower_tile = near_ref[0, 0, 1]
        above = ref[jnp.minimum(upper_tile, tiles - 1)].astype(F32)
        under = ref[jnp.minimum(lower_tile, tiles - 1)].astype(F32)
        above = jnp.where(upper_tile < tiles, above[edge_half : 2 * edge_half], 0.0)
        under = jnp.where(lower_tile < tiles, under[:edge_half], 0.0)
        return above, under

    def repeated(block, count):
        return jnp.concatenate([block] * count, axis=0)

    def write_frame(target, frame, main, top, bottom, hit, full):
        base = LEAD + tall * frame
        target[base : base + columns] = top
        target[base + columns : base + columns + fr] = jnp.where(
            hit, repeated(bottom, height), main
        )
        target[base + columns + fr : base + tall] = jnp.where(full, bottom, 0.0)

    def pad_own(above, under):
        hit = row_id == row_count
        full = row_count[:columns] == height
        for f in range(frames):
            low = columns * f
            write_frame(
                wide,
                f,
                frame_of(flat, f),
                above[low : low + columns],
                under[low : low + columns],
                hit,
                full,
            )

    def make_taps():
        for f in range(frames):
            for row_off in range(3):
                for col_off in range(3):
                    start = LEAD + tall * f + columns * row_off + col_off - 1
                    block = wide[start : start + fr]
                    if col_off == 0:
                        block = jnp.where(column > 0, block, 0.0)
                    if col_off == 2:
                        block = jnp.where(column < columns - 1, block, 0.0)
                    taps_mat[
                        row_off,
                        fr * f : fr * (f + 1),
                        channels * col_off : channels * (col_off + 1),
                    ] = block.astype(BF16)

    def conv_front():
        sums = [jnp.zeros((fr, channels), F32) for _ in range(frames)]
        for depth_off in range(3):
            count = frames - 2 + depth_off
            part = jnp.zeros((fr * count, channels), F32)
            for row_off in range(3):
                tap = 9 * depth_off + 3 * row_off
                part += jnp.dot(
                    taps_mat[row_off, : fr * count, :],
                    weight[tap : tap + 3].reshape(3 * channels, channels),
                    preferred_element_type=F32,
                )
            for n in range(count):
                sums[frames - count + n] += part[fr * n : fr * (n + 1)]
        return sums

    def conv_back():
        sums = [jnp.zeros((fr, channels), F32) for _ in range(frames)]
        for depth_off in range(3):
            count = frames - depth_off
            part = jnp.zeros((fr * count, channels), F32)
            for row_off in range(3):
                for col_off in range(3):
                    tap = 9 * depth_off + 3 * row_off + col_off
                    part += lax.dot_general(
                        taps_mat[
                            row_off,
                            fr * depth_off :,
                            channels * col_off : channels * (col_off + 1),
                        ],
                        weight[26 - tap],
                        (((1,), (1,)), ((), ())),
                        preferred_element_type=F32,
                    )
            for n in range(count):
                sums[n] += part[fr * n : fr * (n + 1)]
        return sums

    def write_out(frame, values):
        for row in range(height):
            out_ref[frame, row] = values[columns * row : columns * (row + 1)].astype(BF16)

    def shares(dest_tile):
        tap, first = share_of(clip, dest_tile, tiles, row_total, channels)
        return tap, jnp.minimum(tap + 1, 8), first

    dests = [tile] + (tile_peers if square else [])

    def make_selections():
        place = lax.broadcasted_iota(jnp.int32, (rows, 128), 0)
        lane = lax.broadcasted_iota(jnp.int32, (rows, 128), 1)
        col_id = place % columns
        line_id = place // columns
        frame_id = line_id // height
        line_id = line_id - height * frame_id
        for dest, dest_tile in enumerate(dests):
            for half_id, tap in enumerate(shares(dest_tile)[:2]):
                row_off, col_off = tap // 3, tap % 3
                row_off = row_off + section * (2 - 2 * row_off) - 1
                col_off = col_off + section * (2 - 2 * col_off) - 1
                there, beyond = line_id + row_off, col_id + col_off
                valid = (beyond >= 0) & (beyond < columns)
                main = jnp.where(
                    valid & (there >= 0) & (there < height),
                    place + columns * row_off + col_off,
                    -1,
                )
                rim = jnp.where(valid, columns * frame_id + beyond, -4 * rows)
                top = jnp.where(there == -1, rim + rows, -1)
                low = rows * half_id
                main_sel[dest, low : low + rows] = jnp.where(lane == main, 1.0, 0.0).astype(BF16)
                rest = (lane + 128 == main) | (lane + 128 == top)
                rest_sel[dest, low : low + rows] = jnp.where(rest, 1.0, 0.0)
                under_sel[dest, low : low + rows] = jnp.where(
                    lane + 128 == rim + rows + edge_half, there.astype(F32), -5.0
                )

    is_encoder = section == 0
    is_decoder = section != 0
    wide[...] = jnp.zeros(wide.shape, F32)
    loads[0].wait()
    loads[1].wait()

    @pl.when(is_encoder)
    def _():
        read_field(video, flat)
        for f in range(frames):
            values = jnp.where(inside, frame_of(flat, f), 0.0)
            active = silu(values).astype(BF16)
            early_all[clip, tile, fr * f : fr * (f + 1)] = active
            flat[fr * f : fr * (f + 1)] = active.astype(F32)

    @pl.when(is_decoder)
    def _():
        read_field(cot, flat)
        for f in range(frames):
            values = jnp.where(inside, frame_of(flat, f), 0.0)
            early_all[clip, tile, fr * f : fr * (f + 1)] = values.astype(BF16)
            flat[fr * f : fr * (f + 1)] = values

    halo_one[tile] = ends_of(flat).astype(BF16)
    pl.semaphore_wait(barrier, len(greeted))
    send_halo(halo_one, 0)
    early.send_own(clip_first)
    make_selections()
    early.send_own(clip_rest)
    early.across(clip)

    loads[3].wait()
    above, under = take_halo(halo_one, 0)
    pad_own(above, under)
    count_rows = row_count[:columns].astype(F32)
    edge_all[clip, tile] = jnp.concatenate(
        [above[: edge_half - columns], count_rows, under], axis=0
    ).astype(BF16)
    edge.send_own(clip_peers)
    edge.across(clip)
    make_taps()
    loads[2].wait()

    @pl.when(is_encoder)
    def _():
        read_field(video, flat)
        sums = conv_front()
        for f in range(frames):
            values = jnp.where(inside, frame_of(flat, f) + sums[f], 0.0).astype(BF16)
            give[fr * f : fr * (f + 1)] = values.astype(F32)

    @pl.when(is_decoder)
    def _():
        sums = conv_back()
        for f in range(frames):
            give[fr * f : fr * (f + 1)] = sums[f]

    swap = pltpu.make_async_remote_copy(
        src_ref=give,
        dst_ref=got,
        send_sem=swap_sem.at[0],
        recv_sem=swap_sem.at[1],
        device_id=twin,
        device_id_type=MESH,
    )
    go(swap)

    @pl.when(is_encoder)
    def _():
        read_field(cot, flat)
        for f in range(frames):
            write_out(f, frame_of(give, f))

    if line:
        early.arrived(over, tile)
        early.along()
        early.across(over)
        early.arrived(near, tile)
        early.across(near)
    swap.wait_recv()

    @pl.when(is_encoder)
    def _():
        for f in range(frames):
            target = frame_of(flat, f)
            values = target + silu_grad(frame_of(give, f)) * frame_of(got, f)
            late_all[clip, tile, fr * f : fr * (f + 1)] = jnp.where(inside, values, 0.0).astype(
                BF16
            )

    @pl.when(is_decoder)
    def _():
        for f in range(frames):
            active = silu(frame_of(got, f)).astype(BF16)
            late_all[clip, tile, fr * f : fr * (f + 1)] = active
            flat[fr * f : fr * (f + 1)] = active.astype(F32)
        halo_two[tile] = ends_of(flat).astype(BF16)

    def make_shift(target, slot, source_tile, dest):
        first = shares(dests[dest])[2]
        lane = lax.broadcasted_iota(jnp.int32, (rows, channels), 1)
        keep_first = (lane >= first) | is_decoder

        @pl.loop(0, clips, unroll=clips if square else 1)
        def _(index):
            rim = edge_all[index, source_tile]
            count = rim.astype(F32)[edge_half - columns : edge_half - columns + 1, :128]
            rest = rest_sel[dest] + jnp.where(under_sel[dest] == count, 1.0, 0.0)
            picks = jnp.concatenate([main_sel[dest], rest.astype(BF16)], axis=1)
            field = jnp.concatenate([early_all[index, source_tile], rim], axis=0)
            moved = jnp.dot(
                picks[:, : rows + 2 * edge_half], field, preferred_element_type=F32
            )
            picked = jnp.where(keep_first, moved[:rows], moved[rows:])
            target[slot, index, :, :channels] = picked.astype(BF16)
            target[slot, index, :, channels:] = moved[rows:].astype(BF16)

    def column_arrived(field, source_tile, side=None):
        for index in range(clips):
            field.arrived(index, source_tile, side)

    def shift_column(number):
        peer = tile_peers[number]
        column_arrived(early, peer)
        column_arrived(edge, peer)
        make_shift(shift_far, 2 * number + 1, peer, 2 - number)
        make_shift(shift_own, number + 1, peer, 0)

    late.send_own(clip_first)
    send_halo(halo_two, 1, is_decoder)
    if line:
        edge.arrived(over, tile)
        edge.along()

    for peer in [far] if line else clip_peers:
        early.arrived(peer, tile)
        early.across(peer)
    for peer in reversed(clip_peers):
        if not (line and peer is over):
            edge.arrived(peer, tile)
        edge.across(peer)

    late.send_own(clip_rest)
    late.across(clip)
    make_shift(shift_own, 0, tile, 0)
    if square:
        for number in range(2):
            make_shift(shift_far, 2 * number, tile, 2 - number)
    for peer in [over, near] if line else clip_peers:
        late.arrived(peer, tile)
        if line and peer is over:
            late.along()
        late.across(peer)

    @pl.when(is_decoder)
    def _():
        pad_own(*take_halo(halo_two, 1))
        make_taps()
        sums = conv_front()
        for f in range(frames):
            write_out(f, jnp.where(inside, frame_of(got, f) + sums[f], 0.0))

    if square:
        shift_column(0)
    if line:
        late.arrived(far, tile)
        late.across(far)
    if square:
        shift_column(1)
    else:
        for number, peer in enumerate(tile_peers):
            column_arrived(early, peer)
            column_arrived(edge, peer)
            make_shift(shift_own, number + 1, peer, 0)

    def stacked(ref, lead, low, count, lanes):
        blocks = [
            ref[lead(index) + (slice(fr * low, fr * (low + count)), lanes)]
            for index in range(clips)
        ]
        return jnp.concatenate(blocks, axis=0)

    contract = (((0,), (0,)), ((), ()))
    whole = slice(0, channels)

    def products(shift, slot, source_tile, dest_tile, tap, side):
        count = frames - 2 + tap
        _, _, first = shares(dest_tile)
        shift_at = lambda index: (slot, index)
        late_at = lambda index: (index, source_tile)
        lanes = whole if side is None else slice(half * side, half * (side + 1))
        width = lanes.stop - lanes.start
        if_encoder = lambda: lax.dot_general(
            stacked(shift, shift_at, 0, count, whole),
            stacked(late_all, late_at, frames - count, count, lanes),
            contract,
            preferred_element_type=F32,
        )

        def if_decoder():
            acts = stacked(late_all, late_at, 0, count, whole)
            sums = [
                lax.dot_general(
                    acts,
                    stacked(
                        shift,
                        shift_at,
                        frames - count,
                        count,
                        slice(base + lanes.start, base + lanes.stop),
                    ),
                    contract,
                    preferred_element_type=F32,
                )
                for base in (0, channels)
            ]
            rows = lax.broadcasted_iota(jnp.int32, (channels, width), 0)
            return jnp.where(rows >= first, sums[0], sums[1])

        return if_encoder, if_decoder

    def keep(tap, low, left, values):
        high, right = low + values.shape[0], left + values.shape[1]
        result[tap, low:high, left:right] = values
        result[tap, channels + low : channels + high, left:right] = values

    def window(tap, dest_tile, width):
        _, _, first = shares(dest_tile)
        if row_total % 16 == 0:
            first = pl.multiple_of(first, 16)
            return result[tap, pl.ds(first, row_total), :width]
        turned = pltpu.roll(result[tap, :channels, :width], (channels - first) % channels, 0)
        return turned[:row_total]

    def half_encoder(sources, tap, side):
        count = frames - 2 + tap
        lanes = slice(half * side, half * (side + 1))
        moved = [
            stacked(ref, lambda index: (slot, index), 0, count, whole) for ref, slot, _ in sources
        ]
        ups = [
            stacked(late_all, lambda index: (index, source), frames - count, count, lanes)
            for _, _, source in sources
        ]
        return lax.dot_general(
            jnp.concatenate(moved, axis=0),
            jnp.concatenate(ups, axis=0),
            contract,
            preferred_element_type=F32,
        )

    def half_decoder(sources, tap, side, first):
        count = frames - 2 + tap
        lanes = slice(half * side, half * (side + 1))
        acts = jnp.concatenate(
            [
                stacked(late_all, lambda index: (index, source), 0, count, lanes)
                for _, _, source in sources
            ],
            axis=0,
        )
        sums = []
        for base in (0, channels):
            moved = [
                stacked(
                    ref,
                    lambda index: (slot, index),
                    frames - count,
                    count,
                    slice(base, base + channels),
                )
                for ref, slot, _ in sources
            ]
            sums.append(
                lax.dot_general(
                    acts,
                    jnp.concatenate(moved, axis=0),
                    contract,
                    preferred_element_type=F32,
                )
            )
        ids = lax.broadcasted_iota(jnp.int32, (half, channels), 0) + half * side
        return jnp.where(ids >= first, sums[0], sums[1])

    def portion(ref, other, side, place):
        return pltpu.make_async_remote_copy(
            src_ref=ref.at[side],
            dst_ref=other.at[side],
            send_sem=part_out.at[side],
            recv_sem=part_in.at[side],
            device_id=place,
            device_id_type=MESH,
        )

    if square:
        for side in range(2):
            peer, dest = tile_peers[side], tile_peers[1 - side]
            column_arrived(late, peer, side)
            sources = [(shift_far, 2 * side, tile), (shift_far, 2 * side + 1, peer)]

            @pl.when(is_encoder)
            def _():
                for tap in range(3):
                    keep(tap, 0, 0, half_encoder(sources, tap, side))
                    part_send[side, tap] = window(tap, dest, half).astype(BF16)

            @pl.when(is_decoder)
            def _():
                first = shares(dest)[2]
                for tap in range(3):
                    values = half_decoder(sources, tap, side, first)
                    rows_send[side, tap] = values.astype(BF16)

            place = (section, clip, dest)
            go(portion(part_send, part_recv, side, place), is_encoder)
            go(portion(rows_send, rows_recv, side, place), is_decoder)

        own_first = shares(tile)[2]
        own_sources = [
            [(shift_own, 0, tile), (shift_own, side + 1, tile_peers[side])] for side in range(2)
        ]

        @pl.when(is_encoder)
        def _():
            for side in range(2):
                for tap in range(3):
                    keep(tap, 0, half * side, half_encoder(own_sources[side], tap, side))
            for side in range(2):
                portion(part_recv, part_recv, side, twin).wait_recv()

        @pl.when(is_decoder)
        def _():
            for side in range(2):
                for tap in range(3):
                    values = half_decoder(own_sources[side], tap, side, own_first)
                    result[tap, half * side : half * (side + 1)] = values
            for side in range(2):
                portion(rows_recv, rows_recv, side, twin).wait_recv()
                for tap in range(3):
                    values = result[tap, half * side : half * (side + 1)]
                    keep(tap, half * side, 0, values + rows_recv[side, tap].astype(F32))

    else:
        for peer in tile_peers:
            column_arrived(late, peer)
        for tap in range(3):
            result[tap, :channels] = jnp.zeros((channels, channels), F32)
            for which, chosen in ((0, is_encoder), (1, is_decoder)):

                @pl.when(chosen)
                def _():
                    @pl.loop(0, tiles)
                    def _(slot):
                        source = (tile + slot) % tiles
                        result[tap, :channels] += products(
                            shift_own, slot, source, tile, tap, None
                        )[which]()

            result[tap, channels : 2 * channels] = result[tap, :channels]

    def write_grads(tap, values):
        for side in range(2):
            low = 2 * row_total * tap + side
            grads_ref[pl.ds(low, row_total, stride=2), :] = values[
                :, half * side : half * (side + 1)
            ]

    if square:

        @pl.when(is_encoder)
        def _():
            for tap in range(3):
                parts = [part_recv[side, tap].astype(F32) for side in range(2)]
                write_grads(tap, window(tap, tile, channels) + jnp.concatenate(parts, axis=1))

        @pl.when(is_decoder)
        def _():
            for tap in range(3):
                write_grads(tap, window(tap, tile, channels))

    else:
        for tap in range(3):
            write_grads(tap, window(tap, tile, channels))

    for copy, only in started:
        if only is None:
            copy.wait_send()
        else:
            pl.when(only)(copy.wait_send)


def place_kernel(out_from, grads_from, out_to, grads_to, sems):
    copies = [
        pltpu.make_async_copy(grads_from, grads_to, sems.at[0]),
        pltpu.make_async_copy(out_from, out_to, sems.at[1]),
    ]
    for copy in copies:
        copy.start()
    for copy in copies:
        copy.wait()


def local(video, cotangent, weights, neighbours, rows_used, cols_used):
    frames, height, columns, channels = video.shape[2:]
    clips, tiles = lax.axis_size("clip"), lax.axis_size("tile")
    row_total = 9 * channels // (clips * tiles)
    rows = frames * height * columns
    dims = (clips, tiles, frames, height, columns, channels, row_total)
    edge_rows = 2 * columns * (frames + 1)
    padded = 2 * LEAD + frames * (height + 2) * columns
    peers = 2 if tiles == 4 else tiles - 1
    count = (clips - 1 + (1 if clips == 4 else 0)) + peers + (clips - 1) * peers
    dma = pltpu.SemaphoreType.DMA
    held = [
        pltpu.with_memory_space_constraint(array, pltpu.HBM)
        for array in (neighbours, video, cotangent, weights)
    ]
    own_out, summed = pl.pallas_call(
        functools.partial(block_kernel, dims),
        out_shape=(
            jax.ShapeDtypeStruct((frames, height, columns, channels), BF16),
            jax.ShapeDtypeStruct((3 * row_total * 2, channels // 2), F32),
        ),
        in_specs=[pl.BlockSpec(memory_space=pltpu.SMEM)] * 2 + [pl.BlockSpec(memory_space=pltpu.HBM)] * 4,
        out_specs=(pl.BlockSpec(memory_space=pltpu.VMEM),) * 2,
        scratch_shapes=[
            pltpu.SMEM((1, 1, 2), jnp.int32),
            pltpu.VMEM((frames, height, columns, channels), BF16),
            pltpu.VMEM((frames, height, columns, channels), BF16),
            pltpu.VMEM((27, channels, channels), BF16),
            pltpu.VMEM((rows, channels), F32),
            pltpu.VMEM((padded, channels), F32),
            pltpu.VMEM((3, 2 * rows, 128), BF16),
            pltpu.VMEM((3, 2 * rows, 128), F32),
            pltpu.VMEM((3, 2 * rows, 128), F32),
            pltpu.VMEM((3, rows, 3 * channels), BF16),
            pltpu.VMEM((clips, tiles, rows, channels), BF16),
            pltpu.VMEM((clips, tiles, edge_rows, channels), BF16),
            pltpu.VMEM((clips, tiles, rows, channels), BF16),
            pltpu.VMEM((tiles, edge_rows, channels), BF16),
            pltpu.VMEM((tiles, edge_rows, channels), BF16),
            pltpu.VMEM((rows, channels), F32),
            pltpu.VMEM((rows, channels), F32),
            pltpu.VMEM((peers + 1, clips, rows, 2 * channels), BF16),
            pltpu.VMEM((4 if tiles == 4 else 1, clips, rows, 2 * channels), BF16),
            pltpu.VMEM((3, 2 * channels, channels), F32),
            pltpu.VMEM((2, 3, row_total, channels // 2), BF16),
            pltpu.VMEM((2, 3, row_total, channels // 2), BF16),
            pltpu.VMEM((2, 3, channels // 2, channels), BF16),
            pltpu.VMEM((2, 3, channels // 2, channels), BF16),
            dma((4,)),
            dma((count,)),
            dma((count,)),
            dma((count,)),
            dma((clips, tiles)),
            dma((clips, tiles)),
            dma((clips, tiles)),
            dma((2, tiles - 1)),
            dma((2, tiles)),
            dma((2,)),
            dma((2,)),
            dma((2,)),
        ],
        compiler_params=pltpu.CompilerParams(
            collective_id=0,
            has_side_effects=True,
            vmem_limit_bytes=(32 if tiles == 4 else 56) * 2**20,
        ),
    )(rows_used, cols_used, *held)
    own_out, summed = pl.pallas_call(
        place_kernel,
        out_shape=(
            jax.ShapeDtypeStruct(own_out.shape, BF16),
            jax.ShapeDtypeStruct(summed.shape, F32),
        ),
        in_specs=[pl.BlockSpec(memory_space=pl.ANY)] * 2,
        out_specs=(pl.BlockSpec(memory_space=pltpu.HBM),) * 2,
        scratch_shapes=[dma((2,))],
        compiler_params=pltpu.CompilerParams(vmem_limit_bytes=2**20),
    )(own_out, summed)
    return (own_out[None, None, None], summed.reshape(1, 3, row_total * channels))


def solution(mesh):
    in_specs = (
        P("clip", "tile", None, None, None, None),
        P("clip", "tile", None, None, None, None),
        P("segment", None, None, None),
        P("clip", "tile", None),
        P("clip", "tile"),
        P("clip"),
    )
    out_specs = (
        P("segment", "clip", "tile", None, None, None, None),
        P("segment", None, ("clip", "tile")),
    )
    return jax.shard_map(local, mesh=mesh, in_specs=in_specs, out_specs=out_specs, check_vma=False)
```

```python
import functools

import jax
import jax.numpy as jnp
from jax import lax
from jax.experimental import pallas as pl
from jax.experimental.pallas import tpu as pltpu
from jax.sharding import PartitionSpec as P

MESH = pl.DeviceIdType.MESH
F32, BF16 = jnp.float32, jnp.bfloat16
LEAD = 8


def silu(values):
    return values / (1.0 + jnp.exp(-values))


def silu_grad(values):
    sigmoid = 1.0 / (1.0 + jnp.exp(-values))
    return sigmoid * (1.0 + values * (1.0 - sigmoid))


def share_of(clip, tile, tiles, row_total, channels):
    start = (clip * tiles + tile) * row_total
    return start // channels, start % channels


def block_kernel(
    dims,
    rows_ref,
    cols_ref,
    near_hbm,
    video_hbm,
    cot_hbm,
    weight_hbm,
    out_ref,
    grads_ref,
    near_ref,
    video,
    cot,
    weight,
    flat,
    wide,
    main_sel,
    rest_sel,
    under_sel,
    taps_mat,
    early_all,
    edge_all,
    late_all,
    halo_one,
    halo_two,
    give,
    got,
    shift_own,
    shift_far,
    result,
    part_send,
    part_recv,
    rows_send,
    rows_recv,
    load_sem,
    early_out,
    edge_out,
    late_out,
    early_in,
    edge_in,
    late_in,
    halo_out,
    halo_in,
    swap_sem,
    part_out,
    part_in,
):
    clips, tiles, frames, height, columns, channels, row_total = dims
    fr = height * columns
    tall = fr + 2 * columns
    rows = frames * fr
    half = channels // 2
    edge_half = columns * (frames + 1)
    section = lax.axis_index("segment")
    clip = lax.axis_index("clip")
    tile = lax.axis_index("tile")
    line = clips == 4
    square = tiles == 4
    inner = (clip + 1) // 2 % 2 == 1

    if line:
        near, over, far = clip + 1 - 2 * (clip % 2), (clip + 2) % 4, 3 - clip
        clip_peers = [over, far, near]
        clip_first, clip_rest = [over], [far, near]
    else:
        clip_peers = [(clip + step) % clips for step in range(1, clips)]
        clip_first, clip_rest = [], clip_peers
    if square:
        beside, below = tile + 1 - 2 * (tile % 2), (tile + 2) % 4
        tile_peers = [beside, below]
        halo_peers = [beside, below, 3 - tile]
    else:
        tile_peers = halo_peers = [(tile + step) % tiles for step in range(1, tiles)]

    loads = [
        pltpu.make_async_copy(cot_hbm.at[0, 0], cot, load_sem.at[0]),
        pltpu.make_async_copy(video_hbm.at[0, 0], video, load_sem.at[1]),
        pltpu.make_async_copy(weight_hbm.at[0], weight, load_sem.at[2]),
        pltpu.make_async_copy(near_hbm, near_ref, load_sem.at[3]),
    ]
    for index in (0, 1, 3, 2):
        loads[index].start()

    twin = (1 - section, clip, tile)
    barrier = pltpu.get_barrier_semaphore()
    greeted = [twin]
    greeted += [(section, peer, tile) for peer in clip_peers]
    greeted += [(section, clip, peer) for peer in halo_peers]
    for place in greeted:
        pl.semaphore_signal(barrier, inc=1, device_id=place, device_id_type=MESH)

    row_count = jnp.full((fr, channels), rows_ref[0, 0], jnp.int32)
    col_count = cols_ref[0]
    ids = lax.broadcasted_iota(jnp.int32, (fr, channels), 0)
    column = ids % columns
    row_id = ids // columns
    inside = (row_id < row_count) & (column < col_count)

    started = []

    def transfer(ref, slot, send_sem, recv_sem, place):
        return pltpu.make_async_remote_copy(
            src_ref=ref.at[slot],
            dst_ref=ref.at[slot],
            send_sem=send_sem,
            recv_sem=recv_sem,
            device_id=place,
            device_id_type=MESH,
        )

    def go(copy, only=None):
        started.append((copy, only))
        if only is None:
            copy.start()
        else:
            pl.when(only)(copy.start)

    class Field:
        def __init__(self, ref, outs, ins, halved=False):
            self.ref, self.outs, self.ins, self.used = ref, outs, ins, 0
            self.halved = halved

        def part(self, slot_clip, slot_tile, side):
            if side is None:
                return slot_clip, slot_tile
            return slot_clip, slot_tile, slice(None), pl.ds(half * side, half)

        def send(self, slot_clip, place, only=None, side=None):
            copy = transfer(
                self.ref,
                self.part(slot_clip, tile, side),
                self.outs.at[self.used],
                self.ins.at[slot_clip, tile],
                place,
            )
            self.used += 1
            go(copy, only)

        def send_own(self, peers):
            for peer in peers:
                skip = line and peer is far
                self.send(clip, (section, peer, tile), inner if skip else None)

        def arrived(self, slot_clip, slot_tile, side=None):
            transfer(
                self.ref,
                self.part(slot_clip, slot_tile, side),
                self.outs.at[0],
                self.ins.at[slot_clip, slot_tile],
                twin,
            ).wait_recv()

        def along(self):
            self.send(over, (section, near, tile), inner)

        def across(self, slot_clip):
            for number, peer in enumerate(tile_peers):
                side = number if self.halved else None
                self.send(slot_clip, (section, clip, peer), None, side)

    early = Field(early_all, early_out, early_in)
    edge = Field(edge_all, edge_out, edge_in)
    late = Field(late_all, late_out, late_in, square)

    def read_field(source, target):
        for frame in range(frames):
            for row in range(height):
                low = fr * frame + columns * row
                target[low : low + columns] = source[frame, row].astype(F32)

    def frame_of(ref, frame):
        return ref[fr * frame : fr * (frame + 1)]

    def ends_of(ref):
        leading = [ref[fr * f : fr * f + columns] for f in range(frames)]
        trailing = []
        for f in range(frames):
            last = leading[f]
            for row in range(1, height):
                low = fr * f + columns * row
                last = jnp.where(row_count[:columns] == row + 1, ref[low : low + columns], last)
            trailing.append(last)
        blank = jnp.zeros((columns, channels), F32)
        return jnp.concatenate(leading + [blank] + trailing + [blank], axis=0)

    def send_halo(ref, number, only=None):
        for index, peer in enumerate(halo_peers):
            copy = transfer(
                ref,
                tile,
                halo_out.at[number, index],
                halo_in.at[number, tile],
                (section, clip, peer),
            )
            go(copy, only)

    def take_halo(ref, number):
        for peer in halo_peers:
            transfer(ref, peer, halo_out.at[number, 0], halo_in.at[number, peer], twin).wait_recv()
        upper_tile = near_ref[0, 0, 0]
        lower_tile = near_ref[0, 0, 1]
        above = ref[jnp.minimum(upper_tile, tiles - 1)].astype(F32)
        under = ref[jnp.minimum(lower_tile, tiles - 1)].astype(F32)
        above = jnp.where(upper_tile < tiles, above[edge_half : 2 * edge_half], 0.0)
        under = jnp.where(lower_tile < tiles, under[:edge_half], 0.0)
        return above, under

    def repeated(block, count):
        return jnp.concatenate([block] * count, axis=0)

    def write_frame(target, frame, main, top, bottom, hit, full):
        base = LEAD + tall * frame
        target[base : base + columns] = top
        target[base + columns : base + columns + fr] = jnp.where(
            hit, repeated(bottom, height), main
        )
        target[base + columns + fr : base + tall] = jnp.where(full, bottom, 0.0)

    def pad_own(above, under):
        hit = row_id == row_count
        full = row_count[:columns] == height
        for f in range(frames):
            low = columns * f
            write_frame(
                wide,
                f,
                frame_of(flat, f),
                above[low : low + columns],
                under[low : low + columns],
                hit,
                full,
            )

    def make_taps():
        for f in range(frames):
            for row_off in range(3):
                for col_off in range(3):
                    start = LEAD + tall * f + columns * row_off + col_off - 1
                    block = wide[start : start + fr]
                    if col_off == 0:
                        block = jnp.where(column > 0, block, 0.0)
                    if col_off == 2:
                        block = jnp.where(column < columns - 1, block, 0.0)
                    taps_mat[
                        row_off,
                        fr * f : fr * (f + 1),
                        channels * col_off : channels * (col_off + 1),
                    ] = block.astype(BF16)

    def conv_front():
        sums = [jnp.zeros((fr, channels), F32) for _ in range(frames)]
        for depth_off in range(3):
            count = frames - 2 + depth_off
            part = jnp.zeros((fr * count, channels), F32)
            for row_off in range(3):
                tap = 9 * depth_off + 3 * row_off
                part += jnp.dot(
                    taps_mat[row_off, : fr * count, :],
                    weight[tap : tap + 3].reshape(3 * channels, channels),
                    preferred_element_type=F32,
                )
            for n in range(count):
                sums[frames - count + n] += part[fr * n : fr * (n + 1)]
        return sums

    def conv_back():
        sums = [jnp.zeros((fr, channels), F32) for _ in range(frames)]
        for depth_off in range(3):
            count = frames - depth_off
            part = jnp.zeros((fr * count, channels), F32)
            for row_off in range(3):
                for col_off in range(3):
                    tap = 9 * depth_off + 3 * row_off + col_off
                    part += lax.dot_general(
                        taps_mat[
                            row_off,
                            fr * depth_off :,
                            channels * col_off : channels * (col_off + 1),
                        ],
                        weight[26 - tap],
                        (((1,), (1,)), ((), ())),
                        preferred_element_type=F32,
                    )
            for n in range(count):
                sums[n] += part[fr * n : fr * (n + 1)]
        return sums

    def write_out(frame, values):
        for row in range(height):
            out_ref[frame, row] = values[columns * row : columns * (row + 1)].astype(BF16)

    def shares(dest_tile):
        tap, first = share_of(clip, dest_tile, tiles, row_total, channels)
        return tap, jnp.minimum(tap + 1, 8), first

    dests = [tile] + (tile_peers if square else [])

    def make_selections():
        place = lax.broadcasted_iota(jnp.int32, (rows, 128), 0)
        lane = lax.broadcasted_iota(jnp.int32, (rows, 128), 1)
        col_id = place % columns
        line_id = place // columns
        frame_id = line_id // height
        line_id = line_id - height * frame_id
        for dest, dest_tile in enumerate(dests):
            for half_id, tap in enumerate(shares(dest_tile)[:2]):
                row_off, col_off = tap // 3, tap % 3
                row_off = row_off + section * (2 - 2 * row_off) - 1
                col_off = col_off + section * (2 - 2 * col_off) - 1
                there, beyond = line_id + row_off, col_id + col_off
                valid = (beyond >= 0) & (beyond < columns)
                main = jnp.where(
                    valid & (there >= 0) & (there < height),
                    place + columns * row_off + col_off,
                    -1,
                )
                rim = jnp.where(valid, columns * frame_id + beyond, -4 * rows)
                top = jnp.where(there == -1, rim + rows, -1)
                low = rows * half_id
                main_sel[dest, low : low + rows] = jnp.where(lane == main, 1.0, 0.0).astype(BF16)
                rest = (lane + 128 == main) | (lane + 128 == top)
                rest_sel[dest, low : low + rows] = jnp.where(rest, 1.0, 0.0)
                under_sel[dest, low : low + rows] = jnp.where(
                    lane + 128 == rim + rows + edge_half, there.astype(F32), -5.0
                )

    is_encoder = section == 0
    is_decoder = section != 0
    wide[...] = jnp.zeros(wide.shape, F32)
    loads[0].wait()
    loads[1].wait()

    @pl.when(is_encoder)
    def _():
        read_field(video, flat)
        for f in range(frames):
            values = jnp.where(inside, frame_of(flat, f), 0.0)
            active = silu(values).astype(BF16)
            early_all[clip, tile, fr * f : fr * (f + 1)] = active
            flat[fr * f : fr * (f + 1)] = active.astype(F32)

    @pl.when(is_decoder)
    def _():
        read_field(cot, flat)
        for f in range(frames):
            values = jnp.where(inside, frame_of(flat, f), 0.0)
            early_all[clip, tile, fr * f : fr * (f + 1)] = values.astype(BF16)
            flat[fr * f : fr * (f + 1)] = values

    halo_one[tile] = ends_of(flat).astype(BF16)
    pl.semaphore_wait(barrier, len(greeted))
    send_halo(halo_one, 0)
    early.send_own(clip_first)
    make_selections()
    early.send_own(clip_rest)
    early.across(clip)

    loads[3].wait()
    above, under = take_halo(halo_one, 0)
    pad_own(above, under)
    count_rows = row_count[:columns].astype(F32)
    edge_all[clip, tile] = jnp.concatenate(
        [above[: edge_half - columns], count_rows, under], axis=0
    ).astype(BF16)
    edge.send_own(clip_peers)
    edge.across(clip)
    make_taps()
    loads[2].wait()

    @pl.when(is_encoder)
    def _():
        read_field(video, flat)
        sums = conv_front()
        for f in range(frames):
            values = jnp.where(inside, frame_of(flat, f) + sums[f], 0.0).astype(BF16)
            give[fr * f : fr * (f + 1)] = values.astype(F32)

    @pl.when(is_decoder)
    def _():
        sums = conv_back()
        for f in range(frames):
            give[fr * f : fr * (f + 1)] = sums[f]

    swap = pltpu.make_async_remote_copy(
        src_ref=give,
        dst_ref=got,
        send_sem=swap_sem.at[0],
        recv_sem=swap_sem.at[1],
        device_id=twin,
        device_id_type=MESH,
    )
    go(swap)

    @pl.when(is_encoder)
    def _():
        read_field(cot, flat)
        for f in range(frames):
            write_out(f, frame_of(give, f))

    if line:
        early.arrived(over, tile)
        early.along()
        early.across(over)
        early.arrived(near, tile)
        early.across(near)
    swap.wait_recv()

    @pl.when(is_encoder)
    def _():
        for f in range(frames):
            target = frame_of(flat, f)
            values = target + silu_grad(frame_of(give, f)) * frame_of(got, f)
            late_all[clip, tile, fr * f : fr * (f + 1)] = jnp.where(inside, values, 0.0).astype(
                BF16
            )

    @pl.when(is_decoder)
    def _():
        for f in range(frames):
            active = silu(frame_of(got, f)).astype(BF16)
            late_all[clip, tile, fr * f : fr * (f + 1)] = active
            flat[fr * f : fr * (f + 1)] = active.astype(F32)
        halo_two[tile] = ends_of(flat).astype(BF16)

    def make_shift(target, slot, source_tile, dest):
        first = shares(dests[dest])[2]
        lane = lax.broadcasted_iota(jnp.int32, (rows, channels), 1)
        keep_first = (lane >= first) | is_decoder

        @pl.loop(0, clips, unroll=clips if square else 1)
        def _(index):
            rim = edge_all[index, source_tile]
            count = rim.astype(F32)[edge_half - columns : edge_half - columns + 1, :128]
            rest = rest_sel[dest] + jnp.where(under_sel[dest] == count, 1.0, 0.0)
            picks = jnp.concatenate([main_sel[dest], rest.astype(BF16)], axis=1)
            field = jnp.concatenate([early_all[index, source_tile], rim], axis=0)
            moved = jnp.dot(
                picks[:, : rows + 2 * edge_half], field, preferred_element_type=F32
            )
            picked = jnp.where(keep_first, moved[:rows], moved[rows:])
            target[slot, index, :, :channels] = picked.astype(BF16)
            target[slot, index, :, channels:] = moved[rows:].astype(BF16)

    def column_arrived(field, source_tile, side=None):
        for index in range(clips):
            field.arrived(index, source_tile, side)

    def shift_column(number):
        peer = tile_peers[number]
        column_arrived(early, peer)
        column_arrived(edge, peer)
        make_shift(shift_far, 2 * number + 1, peer, 2 - number)
        make_shift(shift_own, number + 1, peer, 0)

    late.send_own(clip_first)
    send_halo(halo_two, 1, is_decoder)
    if line:
        edge.arrived(over, tile)
        edge.along()

    for peer in [far] if line else clip_peers:
        early.arrived(peer, tile)
        early.across(peer)
    for peer in reversed(clip_peers):
        if not (line and peer is over):
            edge.arrived(peer, tile)
        edge.across(peer)

    late.send_own(clip_rest)
    late.across(clip)
    make_shift(shift_own, 0, tile, 0)
    if square:
        for number in range(2):
            make_shift(shift_far, 2 * number, tile, 2 - number)
    for peer in [over, near] if line else clip_peers:
        late.arrived(peer, tile)
        if line and peer is over:
            late.along()
        late.across(peer)

    if line:
        late.arrived(far, tile)
        late.across(far)
    if square:
        shift_column(0)
        shift_column(1)
    else:
        for number, peer in enumerate(tile_peers):
            column_arrived(early, peer)
            column_arrived(edge, peer)
            make_shift(shift_own, number + 1, peer, 0)

    def stacked(ref, lead, low, count, lanes):
        blocks = [
            ref[lead(index) + (slice(fr * low, fr * (low + count)), lanes)]
            for index in range(clips)
        ]
        return jnp.concatenate(blocks, axis=0)

    contract = (((0,), (0,)), ((), ()))
    whole = slice(0, channels)

    def products(shift, slot, source_tile, dest_tile, tap, side):
        count = frames - 2 + tap
        _, _, first = shares(dest_tile)
        shift_at = lambda index: (slot, index)
        late_at = lambda index: (index, source_tile)
        lanes = whole if side is None else slice(half * side, half * (side + 1))
        width = lanes.stop - lanes.start
        if_encoder = lambda: lax.dot_general(
            stacked(shift, shift_at, 0, count, whole),
            stacked(late_all, late_at, frames - count, count, lanes),
            contract,
            preferred_element_type=F32,
        )

        def if_decoder():
            acts = stacked(late_all, late_at, 0, count, whole)
            sums = [
                lax.dot_general(
                    acts,
                    stacked(
                        shift,
                        shift_at,
                        frames - count,
                        count,
                        slice(base + lanes.start, base + lanes.stop),
                    ),
                    contract,
                    preferred_element_type=F32,
                )
                for base in (0, channels)
            ]
            rows = lax.broadcasted_iota(jnp.int32, (channels, width), 0)
            return jnp.where(rows >= first, sums[0], sums[1])

        return if_encoder, if_decoder

    def keep(tap, low, left, values):
        high, right = low + values.shape[0], left + values.shape[1]
        result[tap, low:high, left:right] = values
        result[tap, channels + low : channels + high, left:right] = values

    def window(tap, dest_tile, width):
        _, _, first = shares(dest_tile)
        if row_total % 16 == 0:
            first = pl.multiple_of(first, 16)
            return result[tap, pl.ds(first, row_total), :width]
        turned = pltpu.roll(result[tap, :channels, :width], (channels - first) % channels, 0)
        return turned[:row_total]

    def half_encoder(sources, tap, side):
        count = frames - 2 + tap
        lanes = slice(half * side, half * (side + 1))
        moved = [
            stacked(ref, lambda index: (slot, index), 0, count, whole) for ref, slot, _ in sources
        ]
        ups = [
            stacked(late_all, lambda index: (index, source), frames - count, count, lanes)
            for _, _, source in sources
        ]
        return lax.dot_general(
            jnp.concatenate(moved, axis=0),
            jnp.concatenate(ups, axis=0),
            contract,
            preferred_element_type=F32,
        )

    def half_decoder(sources, tap, side, first):
        count = frames - 2 + tap
        lanes = slice(half * side, half * (side + 1))
        acts = jnp.concatenate(
            [
                stacked(late_all, lambda index: (index, source), 0, count, lanes)
                for _, _, source in sources
            ],
            axis=0,
        )
        sums = []
        for base in (0, channels):
            moved = [
                stacked(
                    ref,
                    lambda index: (slot, index),
                    frames - count,
                    count,
                    slice(base, base + channels),
                )
                for ref, slot, _ in sources
            ]
            sums.append(
                lax.dot_general(
                    acts,
                    jnp.concatenate(moved, axis=0),
                    contract,
                    preferred_element_type=F32,
                )
            )
        ids = lax.broadcasted_iota(jnp.int32, (half, channels), 0) + half * side
        return jnp.where(ids >= first, sums[0], sums[1])

    def portion(ref, other, side, place):
        return pltpu.make_async_remote_copy(
            src_ref=ref.at[side],
            dst_ref=other.at[side],
            send_sem=part_out.at[side],
            recv_sem=part_in.at[side],
            device_id=place,
            device_id_type=MESH,
        )

    if square:
        for side in range(2):
            peer, dest = tile_peers[side], tile_peers[1 - side]
            column_arrived(late, peer, side)
            sources = [(shift_far, 2 * side, tile), (shift_far, 2 * side + 1, peer)]

            @pl.when(is_encoder)
            def _():
                for tap in range(3):
                    keep(tap, 0, 0, half_encoder(sources, tap, side))
                    part_send[side, tap] = window(tap, dest, half).astype(BF16)

            @pl.when(is_decoder)
            def _():
                first = shares(dest)[2]
                for tap in range(3):
                    values = half_decoder(sources, tap, side, first)
                    rows_send[side, tap] = values.astype(BF16)

            place = (section, clip, dest)
            go(portion(part_send, part_recv, side, place), is_encoder)
            go(portion(rows_send, rows_recv, side, place), is_decoder)

        @pl.when(is_decoder)
        def _():
            pad_own(*take_halo(halo_two, 1))
            make_taps()
            sums = conv_front()
            for f in range(frames):
                write_out(f, jnp.where(inside, frame_of(got, f) + sums[f], 0.0))

        own_first = shares(tile)[2]
        own_sources = [
            [(shift_own, 0, tile), (shift_own, side + 1, tile_peers[side])] for side in range(2)
        ]

        @pl.when(is_encoder)
        def _():
            for side in range(2):
                for tap in range(3):
                    keep(tap, 0, half * side, half_encoder(own_sources[side], tap, side))
            for side in range(2):
                portion(part_recv, part_recv, side, twin).wait_recv()

        @pl.when(is_decoder)
        def _():
            for side in range(2):
                for tap in range(3):
                    values = half_decoder(own_sources[side], tap, side, own_first)
                    result[tap, half * side : half * (side + 1)] = values
            for side in range(2):
                portion(rows_recv, rows_recv, side, twin).wait_recv()
                for tap in range(3):
                    values = result[tap, half * side : half * (side + 1)]
                    keep(tap, half * side, 0, values + rows_recv[side, tap].astype(F32))

    else:

        @pl.when(is_decoder)
        def _():
            pad_own(*take_halo(halo_two, 1))
            make_taps()
            sums = conv_front()
            for f in range(frames):
                write_out(f, jnp.where(inside, frame_of(got, f) + sums[f], 0.0))

        for peer in tile_peers:
            column_arrived(late, peer)
        for tap in range(3):
            result[tap, :channels] = jnp.zeros((channels, channels), F32)
            for which, chosen in ((0, is_encoder), (1, is_decoder)):

                @pl.when(chosen)
                def _():
                    @pl.loop(0, tiles)
                    def _(slot):
                        source = (tile + slot) % tiles
                        result[tap, :channels] += products(
                            shift_own, slot, source, tile, tap, None
                        )[which]()

            result[tap, channels : 2 * channels] = result[tap, :channels]

    def write_grads(tap, values):
        for side in range(2):
            low = 2 * row_total * tap + side
            grads_ref[pl.ds(low, row_total, stride=2), :] = values[
                :, half * side : half * (side + 1)
            ]

    if square:

        @pl.when(is_encoder)
        def _():
            for tap in range(3):
                parts = [part_recv[side, tap].astype(F32) for side in range(2)]
                write_grads(tap, window(tap, tile, channels) + jnp.concatenate(parts, axis=1))

        @pl.when(is_decoder)
        def _():
            for tap in range(3):
                write_grads(tap, window(tap, tile, channels))

    else:
        for tap in range(3):
            write_grads(tap, window(tap, tile, channels))

    for copy, only in started:
        if only is None:
            copy.wait_send()
        else:
            pl.when(only)(copy.wait_send)


def place_kernel(out_from, grads_from, out_to, grads_to, sems):
    copies = [
        pltpu.make_async_copy(grads_from, grads_to, sems.at[0]),
        pltpu.make_async_copy(out_from, out_to, sems.at[1]),
    ]
    for copy in copies:
        copy.start()
    for copy in copies:
        copy.wait()


def local(video, cotangent, weights, neighbours, rows_used, cols_used):
    frames, height, columns, channels = video.shape[2:]
    clips, tiles = lax.axis_size("clip"), lax.axis_size("tile")
    row_total = 9 * channels // (clips * tiles)
    rows = frames * height * columns
    dims = (clips, tiles, frames, height, columns, channels, row_total)
    edge_rows = 2 * columns * (frames + 1)
    padded = 2 * LEAD + frames * (height + 2) * columns
    peers = 2 if tiles == 4 else tiles - 1
    count = (clips - 1 + (1 if clips == 4 else 0)) + peers + (clips - 1) * peers
    dma = pltpu.SemaphoreType.DMA
    held = [
        pltpu.with_memory_space_constraint(array, pltpu.HBM)
        for array in (neighbours, video, cotangent, weights)
    ]
    own_out, summed = pl.pallas_call(
        functools.partial(block_kernel, dims),
        out_shape=(
            jax.ShapeDtypeStruct((frames, height, columns, channels), BF16),
            jax.ShapeDtypeStruct((3 * row_total * 2, channels // 2), F32),
        ),
        in_specs=[pl.BlockSpec(memory_space=pltpu.SMEM)] * 2 + [pl.BlockSpec(memory_space=pltpu.HBM)] * 4,
        out_specs=(pl.BlockSpec(memory_space=pltpu.VMEM),) * 2,
        scratch_shapes=[
            pltpu.SMEM((1, 1, 2), jnp.int32),
            pltpu.VMEM((frames, height, columns, channels), BF16),
            pltpu.VMEM((frames, height, columns, channels), BF16),
            pltpu.VMEM((27, channels, channels), BF16),
            pltpu.VMEM((rows, channels), F32),
            pltpu.VMEM((padded, channels), F32),
            pltpu.VMEM((3, 2 * rows, 128), BF16),
            pltpu.VMEM((3, 2 * rows, 128), F32),
            pltpu.VMEM((3, 2 * rows, 128), F32),
            pltpu.VMEM((3, rows, 3 * channels), BF16),
            pltpu.VMEM((clips, tiles, rows, channels), BF16),
            pltpu.VMEM((clips, tiles, edge_rows, channels), BF16),
            pltpu.VMEM((clips, tiles, rows, channels), BF16),
            pltpu.VMEM((tiles, edge_rows, channels), BF16),
            pltpu.VMEM((tiles, edge_rows, channels), BF16),
            pltpu.VMEM((rows, channels), F32),
            pltpu.VMEM((rows, channels), F32),
            pltpu.VMEM((peers + 1, clips, rows, 2 * channels), BF16),
            pltpu.VMEM((4 if tiles == 4 else 1, clips, rows, 2 * channels), BF16),
            pltpu.VMEM((3, 2 * channels, channels), F32),
            pltpu.VMEM((2, 3, row_total, channels // 2), BF16),
            pltpu.VMEM((2, 3, row_total, channels // 2), BF16),
            pltpu.VMEM((2, 3, channels // 2, channels), BF16),
            pltpu.VMEM((2, 3, channels // 2, channels), BF16),
            dma((4,)),
            dma((count,)),
            dma((count,)),
            dma((count,)),
            dma((clips, tiles)),
            dma((clips, tiles)),
            dma((clips, tiles)),
            dma((2, tiles - 1)),
            dma((2, tiles)),
            dma((2,)),
            dma((2,)),
            dma((2,)),
        ],
        compiler_params=pltpu.CompilerParams(
            collective_id=0,
            has_side_effects=True,
            vmem_limit_bytes=(32 if tiles == 4 else 56) * 2**20,
        ),
    )(rows_used, cols_used, *held)
    own_out, summed = pl.pallas_call(
        place_kernel,
        out_shape=(
            jax.ShapeDtypeStruct(own_out.shape, BF16),
            jax.ShapeDtypeStruct(summed.shape, F32),
        ),
        in_specs=[pl.BlockSpec(memory_space=pl.ANY)] * 2,
        out_specs=(pl.BlockSpec(memory_space=pltpu.HBM),) * 2,
        scratch_shapes=[dma((2,))],
        compiler_params=pltpu.CompilerParams(vmem_limit_bytes=2**20),
    )(own_out, summed)
    return (own_out[None, None, None], summed.reshape(1, 3, row_total * channels))


def solution(mesh):
    in_specs = (
        P("clip", "tile", None, None, None, None),
        P("clip", "tile", None, None, None, None),
        P("segment", None, None, None),
        P("clip", "tile", None),
        P("clip", "tile"),
        P("clip"),
    )
    out_specs = (
        P("segment", "clip", "tile", None, None, None, None),
        P("segment", None, ("clip", "tile")),
    )
    return jax.shard_map(local, mesh=mesh, in_specs=in_specs, out_specs=out_specs, check_vma=False)
```
